32 devices in a mesh: atoms: 8 (over z, y), waves: 4 (over x, core).
Axes of the slice: x: 2, y: 2, z: 4, core: 2. Of those that a mesh axis runs over, the one named last changes fastest.
Arguments:
- features: bfloat16 [2048, 512], P('atoms'), may hold values from -6 to 6
- positions: int32 [3, 2048], P(None, 'atoms'), may hold values from 0 to 65535
- neighbours: int32 [16, 12], P('atoms'), may hold values from 0 to 15, as said below
- wavevectors: int32 [3, 4096], P(None, 'waves'), may hold values from -16 to 16
- radial_width: float32 [8], P('waves'), may hold values from 0.05 to 0.3
- short_weight: bfloat16 [8, 512, 512], P('waves'), may hold values from -0.09375 to 0.09375
- latent_weight: bfloat16 [512, 256], replicated, may hold values from -0.25 to 0.25
- mix_weight: float32 [256, 256], replicated, may hold values from -0.375 to 0.375
- filter_rate: float32 [256], replicated, may hold values from 0.0005 to 0.02
- out_weight: bfloat16 [256, 512], replicated, may hold values from -0.375 to 0.375
Outputs:
- message: bfloat16 [2048, 512], P('atoms', 'waves')
The draws below stay inside these ranges and needn't reach their ends.
Inputs may be any that keep to these rules, and one draw needn't show every extreme that they name: `neighbours`: row b holds 12 different block numbers, each within 7 blocks of b counted cyclically over the 16 blocks; b itself may appear.
All inputs are finite; a program needn't handle non-finite values.
Results may differ from the reference program's by a relative error of at most 0.012.
Values may be sent and summed in bfloat16 or wider, within the bound.
A program may use at most 64 MiB of HBM per device.

```python
import math
import jax
import jax.numpy as jnp
from jax import lax

C = 512
LAT = 256
K = 4096
RADIAL = 8
BLOCK = 128
NBR = 12
REACH = 7
NBLOCKS = 16
NATOMS = 2048
N_WAVES = 4


def draw_neighbours(key, part):
    pop_key, pick_key = jax.random.split(jax.random.fold_in(key, 11))
    span = 2 * REACH + 1
    popularity = jax.random.randint(pop_key, (NBLOCKS,), 0, 4096)
    jitter = jax.random.randint(pick_key, (NBLOCKS, span), 0, 1024)
    shifts = jnp.arange(span, dtype=jnp.int32) - REACH
    block_ids = jnp.arange(NBLOCKS, dtype=jnp.int32)
    target = jnp.mod(block_ids[:, None] + shifts[None, :], NBLOCKS)
    scores = (jitter + popularity[target]) * 32 + (shifts[None, :] + REACH)
    _, picked = lax.top_k(-scores, NBR)
    return jnp.take_along_axis(target, picked, axis=1).astype(jnp.int32)


def with_ends(entries, stream_key, smallest, high):
    place = [jax.random.randint(jax.random.fold_in(stream_key, axis), (), 0, length) for axis, length in enumerate(entries.shape)]
    widest = entries.shape.index(max(entries.shape))
    beside = place[:widest] + [(place[widest] + 1) % entries.shape[widest]] + place[widest + 1:]
    return entries.at[tuple(place)].set(smallest).at[tuple(beside)].set(high)


def shard_levels(key, shape, shards, least, top_value):
    def one(position, shards_of):
        heights = jax.random.uniform(jax.random.fold_in(jax.random.fold_in(key, 6), position), (shards_of,), jnp.float32, least / len(shards), top_value / len(shards))
        return jnp.repeat(jnp.exp(heights), shape[position] // shards_of).reshape((-1,) + (1,) * (len(shape) - position - 1))

    level = one(*shards[0])
    for cut in shards[1:]:
        level = level * one(*cut)
    return level


def noise(stream_key, dims, deviation, reach, pieces=(), kind=jnp.bfloat16):
    values = jax.random.normal(stream_key, dims, jnp.float32) * deviation
    if len(pieces) > 0:
        values = shard_levels(stream_key, dims, pieces, -0.22, 0.18) * values
    return jnp.clip(values, min=-reach, max=reach).astype(kind)


def setup_inputs(seed: int = 0) -> dict:
    key_list = jax.random.split(jax.random.key(seed), 11)
    features = noise(key_list[0], (NATOMS, C), 1.0, 6.0, ((0, 8),))
    positions = with_ends(jax.random.randint(key_list[1], (3, NATOMS), 0, 65536), jax.random.fold_in(key_list[1], 1), 0, 65535).astype(jnp.int32)
    neighbours = draw_neighbours(jax.random.fold_in(key_list[10], 71), 0)
    wavevectors = with_ends(jax.random.randint(key_list[3], (3, K), -16, 17), jax.random.fold_in(key_list[3], 1), -16, 16).astype(jnp.int32)
    radial_width = jnp.clip(jnp.exp(math.log(0.3) - 1.7917595 * jax.random.uniform(key_list[4], (RADIAL,), jnp.float32) ** shard_levels(key_list[4], (RADIAL,), ((0, 4),), -0.2, 0.2)), 0.05, 0.3)
    short_weight = noise(key_list[5], (RADIAL, C, C), (RADIAL * C) ** -0.5, 0.09375, ((0, 4),))
    latent_weight = noise(key_list[6], (C, LAT), C ** -0.5, 0.25)
    mix_weight = noise(key_list[7], (LAT, LAT), LAT ** -0.5, 0.375, (), jnp.float32)
    filter_rate = jnp.clip(jnp.exp(jax.random.uniform(key_list[8], (LAT,), jnp.float32, math.log(0.0005), math.log(0.02))), 0.0005, 0.02)
    out_weight = noise(key_list[9], (LAT, C), LAT ** -0.5, 0.375)
    return dict(features=features, positions=positions, neighbours=neighbours, wavevectors=wavevectors, radial_width=radial_width, short_weight=short_weight, latent_weight=latent_weight, mix_weight=mix_weight, filter_rate=filter_rate, out_weight=out_weight)


cutoff = 0.5

def kernels(own_pos, near_pos, centers, radial_width):
    offsets = own_pos[:, None, :, None] - near_pos[:, :, None, :]
    offsets = jnp.mod(offsets, 65536)
    offsets = jnp.where(offsets >= 32768, offsets - 65536, offsets)
    coords = offsets.astype(jnp.float32) * (1.0 / 65536.0)
    dist_sq = lax.optimization_barrier(jnp.sum(coords * coords, axis=0))
    distance = jnp.sqrt(dist_sq)
    smooth = jnp.where(dist_sq < cutoff * cutoff, jnp.square(1.0 - dist_sq / (cutoff * cutoff)), 0.0)
    shaped = (distance[None] - centers[:, None, None, None]) / radial_width[:, None, None, None]
    norm_scale = 1.0 / math.sqrt(NBR * BLOCK)
    return (jnp.exp(-jnp.square(shaped)) * smooth[None] * norm_scale).astype(jnp.bfloat16)

def phases_of(wavevectors, spots):
    phase_turn = wavevectors[0][:, None] * spots[0][None, :] + wavevectors[1][:, None] * spots[1][None, :] + wavevectors[2][:, None] * spots[2][None, :]
    phase_turn = jnp.mod(phase_turn, 65536)
    angles = phase_turn.astype(jnp.float32) * (2.0 * math.pi / 65536.0)
    return jnp.concatenate([jnp.cos(angles), jnp.sin(angles)], axis=0).astype(jnp.bfloat16)

def filter_gain(wavevectors, filter_rate):
    lengths = lax.optimization_barrier(jnp.sum(wavevectors * wavevectors, axis=0)).astype(jnp.float32)
    return jnp.exp(-lengths[:, None] * filter_rate[None, :])

def reference(features, positions, neighbours, wavevectors, radial_width, short_weight, latent_weight, mix_weight, filter_rate, out_weight):
    block_count = neighbours.shape[0]
    feat_blocks = features.reshape(block_count, BLOCK, C)
    pos_blocks = positions.reshape(3, block_count, BLOCK)
    centers = cutoff * jnp.arange(RADIAL).astype(jnp.float32) / (RADIAL - 1)
    flat_weight = short_weight.reshape(RADIAL * C, C)

    def short_block(block_index):
        near_blocks = neighbours[block_index]
        near_feat = feat_blocks[near_blocks]
        near_pos = pos_blocks[:, near_blocks]
        weights = kernels(pos_blocks[:, block_index], near_pos, centers, radial_width)
        gathered = jnp.einsum('rjia,jac->irc', weights.astype(jnp.float32), near_feat.astype(jnp.float32))
        gathered = gathered.astype(jnp.bfloat16).reshape(BLOCK, RADIAL * C)
        return jnp.dot(gathered, flat_weight, preferred_element_type=jnp.float32)
    block_ids = jnp.arange(block_count, dtype=jnp.int32)
    short_range = lax.map(short_block, block_ids).reshape(block_count * BLOCK, C)
    latent = jnp.dot(features, latent_weight, preferred_element_type=jnp.float32).astype(jnp.bfloat16)
    lat_blocks = latent.reshape(block_count, BLOCK, LAT)

    def add_factor(running, block_index):
        phases = phases_of(wavevectors, pos_blocks[:, block_index])
        return (running + jnp.dot(phases, lat_blocks[block_index], preferred_element_type=jnp.float32), None)
    factors, _ = lax.scan(add_factor, jnp.zeros((2 * K, LAT), jnp.float32), block_ids)
    gain = filter_gain(wavevectors, filter_rate)
    gain = jnp.concatenate([gain, gain], axis=0)
    norm_scale = 1.0 / math.sqrt(block_count * BLOCK)
    mixed = jnp.dot(factors, mix_weight, precision=lax.Precision.HIGHEST)
    filtered = (gain * mixed * norm_scale).astype(jnp.bfloat16)
    group_size = K // N_WAVES

    def long_block(block_index):
        phases = phases_of(wavevectors, pos_blocks[:, block_index])
        running = jnp.zeros((BLOCK, C), jnp.float32)
        for wave_group in range(N_WAVES):
            low = wave_group * group_size
            group_rows = jnp.concatenate([phases[low:low + group_size], phases[K + low:K + low + group_size]], axis=0)
            group_filter = jnp.concatenate([filtered[low:low + group_size], filtered[K + low:K + low + group_size]], axis=0)
            summed = lax.dot_general(group_rows, group_filter, (((0,), (0,)), ((), ())), preferred_element_type=jnp.float32)
            summed = (summed * (1.0 / math.sqrt(K))).astype(jnp.bfloat16)
            running = running + jnp.dot(summed, out_weight, preferred_element_type=jnp.float32)
        return running
    long_range = lax.map(long_block, block_ids).reshape(block_count * BLOCK, C)
    return (short_range + long_range).astype(jnp.bfloat16)
```

```python
import functools
import math

import jax
import jax.numpy as jnp
from jax import lax
from jax.experimental import pallas as pl
from jax.experimental.pallas import tpu as pltpu
from jax.sharding import PartitionSpec as P

K = 4096
RADIAL = 8
BLOCK = 128
NBR = 12
REACH = 7


cutoff = 0.5


def shifted(value, axis, steps):
    count = lax.axis_size(axis)
    pairs = [(source, (source + steps) % count) for source in range(count)]
    return lax.ppermute(value, axis, pairs)


def kernels(own_pos, near_pos, centers, radial_width):
    offsets = own_pos[:, None, :, None] - near_pos[:, :, None, :]
    offsets = jnp.mod(offsets, 65536)
    offsets = jnp.where(offsets >= 32768, offsets - 65536, offsets)
    coords = offsets.astype(jnp.float32) * (1.0 / 65536.0)
    dist_sq = jnp.sum(coords * coords, axis=0)
    distance = jnp.sqrt(dist_sq)
    smooth = jnp.where(
        dist_sq < cutoff * cutoff, jnp.square(1.0 - dist_sq / (cutoff * cutoff)), 0.0
    )
    shaped = (distance[None] - centers[:, None, None, None]) / radial_width[:, None, None, None]
    norm_scale = 1.0 / math.sqrt(NBR * BLOCK)
    return (jnp.exp(-jnp.square(shaped)) * smooth[None] * norm_scale).astype(jnp.bfloat16)


def phases_of(wavevectors, spots):
    phase_turn = (
        wavevectors[0][:, None] * spots[0][None, :]
        + wavevectors[1][:, None] * spots[1][None, :]
        + wavevectors[2][:, None] * spots[2][None, :]
    )
    phase_turn = jnp.mod(phase_turn, 65536)
    angles = phase_turn.astype(jnp.float32) * (2.0 * math.pi / 65536.0)
    return jnp.concatenate([jnp.cos(angles), jnp.sin(angles)], axis=0).astype(jnp.bfloat16)


def filter_gain(wavevectors, filter_rate):
    lengths = jnp.sum(wavevectors * wavevectors, axis=0).astype(jnp.float32)
    return jnp.exp(-lengths[:, None] * filter_rate[None, :])


def local(
    features,
    positions,
    neighbours,
    wavevectors,
    radial_width,
    short_weight,
    latent_weight,
    mix_weight,
    filter_rate,
    out_weight,
):
    row_count = features.shape[0]
    channels = features.shape[1]
    blocks_here = row_count // BLOCK
    atom_devices = lax.axis_size("atoms")
    total_blocks = blocks_here * atom_devices
    reach_hops = -(-REACH // blocks_here)
    window_feat = []
    window_pos = []
    for offset in range(-reach_hops, reach_hops + 1):
        if offset == 0:
            arrived = (features, positions)
        else:
            arrived = shifted((features, positions), "atoms", -offset)
        window_feat.append(arrived[0])
        window_pos.append(arrived[1])
    window_feat = jnp.concatenate(window_feat, axis=0).reshape(-1, BLOCK, channels)
    window_pos = jnp.concatenate(window_pos, axis=1).reshape(3, -1, BLOCK)
    first_block = lax.axis_index("atoms") * blocks_here - reach_hops * blocks_here
    local_near = jnp.mod(neighbours - first_block, total_blocks)
    own_pos = positions.reshape(3, blocks_here, BLOCK)
    local_kernels = radial_width.shape[0]
    kernel_ids = lax.axis_index("waves") * local_kernels + jnp.arange(
        local_kernels, dtype=jnp.int32
    )
    centers = cutoff * kernel_ids.astype(jnp.float32) / (RADIAL - 1)
    flat_weight = short_weight.reshape(local_kernels * channels, channels)

    def short_block(block_index):
        near_blocks = local_near[block_index]
        near_feat = jnp.stack(
            [lax.dynamic_index_in_dim(window_feat, near_blocks[j], 0, False) for j in range(NBR)]
        )
        near_pos = jnp.stack(
            [lax.dynamic_index_in_dim(window_pos, near_blocks[j], 1, False) for j in range(NBR)],
            axis=1,
        )
        weights = kernels(own_pos[:, block_index], near_pos, centers, radial_width)
        gathered = jnp.einsum(
            "rjia,jac->irc", weights, near_feat, preferred_element_type=jnp.float32
        )
        gathered = gathered.astype(jnp.bfloat16).reshape(BLOCK, local_kernels * channels)
        return jnp.dot(gathered, flat_weight, preferred_element_type=jnp.float32)

    short_range = lax.map(short_block, jnp.arange(blocks_here, dtype=jnp.int32)).reshape(
        row_count, channels
    )
    latent = jnp.dot(features, latent_weight, preferred_element_type=jnp.float32).astype(
        jnp.bfloat16
    )
    phases = phases_of(wavevectors, positions)
    partial_factors = jnp.dot(phases, latent, preferred_element_type=jnp.float32)
    gain = filter_gain(wavevectors, filter_rate)
    gain = jnp.concatenate([gain, gain], axis=0)
    norm_scale = 1.0 / math.sqrt(row_count * atom_devices)
    factors = lax.psum(partial_factors, "atoms")
    mixed = jnp.dot(factors, mix_weight, precision=lax.Precision.HIGHEST)
    filtered = (gain * mixed * norm_scale).astype(jnp.bfloat16)
    summed = lax.dot_general(
        phases, filtered, (((0,), (0,)), ((), ())), preferred_element_type=jnp.float32
    )
    summed = (summed * (1.0 / math.sqrt(K))).astype(jnp.bfloat16)
    long_range = jnp.dot(summed, out_weight, preferred_element_type=jnp.float32)
    combined = lax.psum_scatter(
        (short_range + long_range).astype(jnp.bfloat16), "waves", scatter_dimension=1, tiled=True
    )
    return combined


MESH = pl.DeviceIdType.MESH
PIECES = 4
VMEM_LIMIT = 67043328
HALF_SINE = (4.44153573, -7.26468112, 3.2520508)
HALF_COSINE = (1.41449234, -6.98577464, 5.77484937, -1.8561312)
ROOT_LOG2E = math.sqrt(math.log2(math.e))


def cos_sin(turn):
    turn = turn - jnp.round(turn)
    square = turn * turn
    half_sine = HALF_SINE[-1] * square + HALF_SINE[-2]
    half_sine = (half_sine * square + HALF_SINE[0]) * turn
    half_cosine = HALF_COSINE[-1] * square + HALF_COSINE[-2]
    half_cosine = half_cosine * square + HALF_COSINE[1]
    half_cosine = half_cosine * square + HALF_COSINE[0]
    return (
        (1.0 - half_sine * half_sine).astype(jnp.bfloat16),
        (half_sine * half_cosine).astype(jnp.bfloat16),
    )


def turned(rows):
    padded = jnp.concatenate([rows, jnp.zeros((5, rows.shape[1]), jnp.float32)], axis=0)
    return padded.T


def fused_kernel(
    n,
    groups,
    feat_ref,
    pos_ref,
    nbr_ref,
    wave_in,
    width_ref,
    short_in,
    latw_in,
    mix_in,
    rate_in,
    outw_in,
    out_ref,
    wave_ref,
    short_ref,
    latw_ref,
    mix_ref,
    rate_ref,
    outw_ref,
    feat_buf,
    pos_buf,
    fused_w,
    factors,
    gathered,
    wave_cols,
    spot_cols,
    keep_ref,
    gain_ref,
    own_turned,
    filt_buf,
    send_buf,
    recv_buf,
    *rest,
):
    phase_refs, rest = rest[:n], rest[n:]
    weight_refs, rest = rest[:n], rest[n:]
    latent_refs, rest = rest[:n], rest[n:]
    (
        own_sem,
        line_up,
        line_down,
        line_recv,
        side_send,
        side_recv,
        fwd_send,
        fwd_recv,
        pos_up,
        pos_down,
        pos_line,
        pos_side_send,
        pos_side,
        msg_send,
        msg_recv,
    ) = rest
    me = lax.axis_index("atoms")
    group = lax.axis_index("waves")
    core = lax.rem(group, 2)
    partner = group + 1 - 2 * core
    half, channels = feat_ref.shape[1] * feat_ref.shape[2], feat_ref.shape[3]
    rows = 2 * half
    blocks_here = rows // BLOCK
    local_kernels = short_ref.shape[0]
    waves_each = wave_ref.shape[1]
    lines = n // 2
    line, side = me // 2, lax.rem(me, 2)
    can_up, can_down = line < lines - 1, line > 0

    def ranked(rank):
        closest = jnp.minimum(line, lines - 1 - line)
        away = (rank + 1) // 2
        near_line = jnp.where(lax.rem(rank, 2) == 1, line - away, line + away)
        far_line = jnp.where(line < lines - 1 - line, rank, lines - 1 - rank)
        return jnp.where(rank <= 2 * closest, near_line, far_line)

    def remote(piece, send_sem, recv_sem, device):
        return pltpu.make_async_remote_copy(
            src_ref=piece[0],
            dst_ref=piece[1],
            send_sem=send_sem,
            recv_sem=recv_sem,
            device_id=device,
            device_id_type=MESH,
        )

    to_up, to_down = {"atoms": me + 2}, {"atoms": me - 2}
    to_side, to_core = {"atoms": me + 1 - 2 * side}, {"waves": partner}

    def feat_piece(shard_line, shard_side, which):
        place = feat_buf.at[2 * shard_line + shard_side, core, which]
        return place, place

    def own_piece(which):
        return feat_ref.at[core, which], feat_buf.at[me, core, which]

    def pos_piece(shard_line):
        place = pos_buf.at[2 * shard_line + side]
        return place, place

    own_pos_piece = (pos_ref, pos_buf.at[me])

    def up_copy(piece, slot):
        return remote(piece, line_up.at[slot], line_recv.at[slot], to_up)

    def down_copy(piece, slot):
        return remote(piece, line_down.at[slot], line_recv.at[slot], to_down)

    def side_copy(piece, slot):
        return remote(piece, side_send.at[slot], side_recv.at[slot], to_side)

    def forward_copy(shard_line, shard_side, which):
        slot = (2 * shard_line + shard_side) * PIECES + which
        return remote(
            feat_piece(shard_line, shard_side, which), fwd_send.at[slot], fwd_recv.at[slot], to_core
        )

    def pos_up_copy(piece, shard):
        return remote(piece, pos_up.at[shard], pos_line.at[shard], to_up)

    def pos_down_copy(piece, shard):
        return remote(piece, pos_down.at[shard], pos_line.at[shard], to_down)

    def pos_side_copy(piece, shard):
        return remote(piece, pos_side_send.at[shard], pos_side.at[shard], to_side)

    def msg_copy(step):
        target = lax.rem(group + step, groups)
        return remote(
            (send_buf.at[target], recv_buf.at[step]),
            msg_send.at[step],
            msg_recv.at[step],
            {"waves": target},
        )

    own_feat = pltpu.make_async_copy(feat_ref, feat_buf.at[me], own_sem.at[0])
    own_pos = pltpu.make_async_copy(pos_ref, pos_buf.at[me], own_sem.at[1])
    loads = [
        pltpu.make_async_copy(held, kept, own_sem.at[2 + which])
        for which, (held, kept) in enumerate(
            (
                (wave_in, wave_ref),
                (mix_in, mix_ref),
                (latw_in, latw_ref),
                (rate_in, rate_ref),
                (short_in, short_ref),
                (outw_in, outw_ref),
            )
        )
    ]

    barrier = pltpu.get_barrier_semaphore()

    @pl.when(can_up)
    def _():
        pl.semaphore_signal(barrier, inc=1, device_id=to_up, device_id_type=MESH)

    @pl.when(can_down)
    def _():
        pl.semaphore_signal(barrier, inc=1, device_id=to_down, device_id_type=MESH)

    pl.semaphore_signal(barrier, inc=1, device_id=to_side, device_id_type=MESH)
    for step in range(1, groups):
        pl.semaphore_signal(
            barrier,
            inc=1,
            device_id={"waves": lax.rem(group + step, groups)},
            device_id_type=MESH,
        )
    own_pos.start()
    for load in loads[:4]:
        load.start()
    own_feat.start()
    for load in loads[4:]:
        load.start()
    pl.semaphore_wait(
        barrier, groups + jnp.where(can_up, 1, 0) + jnp.where(can_down, 1, 0)
    )

    @pl.when(can_up)
    def _():
        pos_up_copy(own_pos_piece, line).start()

    @pl.when(can_down)
    def _():
        pos_down_copy(own_pos_piece, line).start()

    pos_side_copy(own_pos_piece, line).start()
    for which in range(PIECES):
        slot = line * PIECES + which

        @pl.when(can_up)
        def _():
            up_copy(own_piece(which), slot).start()

        @pl.when(can_down)
        def _():
            down_copy(own_piece(which), slot).start()

        side_copy(own_piece(which), slot).start()

    def pass_on(shard_line, which, upward):
        piece = feat_piece(shard_line, side, which)
        slot = shard_line * PIECES + which
        up_copy(piece, slot).wait_recv()
        if upward:

            @pl.when(can_up)
            def _():
                up_copy(piece, slot).start()

        else:

            @pl.when(can_down)
            def _():
                down_copy(piece, slot).start()

        forward_copy(shard_line, side, which).start()

    def pass_pos(shard_line, upward):
        piece = pos_piece(shard_line)
        pos_up_copy(piece, shard_line).wait_recv()
        if upward:

            @pl.when(can_up)
            def _():
                pos_up_copy(piece, shard_line).start()

        else:

            @pl.when(can_down)
            def _():
                pos_down_copy(piece, shard_line).start()

        pos_side_copy(piece, shard_line).start()

    def at_distance(distance, act):
        @pl.when(line >= distance)
        def _():
            act(line - distance, True)

        @pl.when(line < lines - distance)
        def _():
            act(line + distance, False)

    wave_part = waves_each // PIECES
    row_part = rows // PIECES

    def phase_part(order, origin, part):
        position = pos_buf[origin]
        high = position >> 8
        low = position - (high << 8)
        split = jnp.concatenate(
            [
                high.astype(jnp.float32) * (1.0 / 256.0),
                low.astype(jnp.float32) * (1.0 / 65536.0),
                jnp.zeros((2, rows), jnp.float32),
            ],
            axis=0,
        ).astype(jnp.bfloat16)
        begin = pl.multiple_of(part * wave_part, wave_part)
        turn = jnp.dot(
            wave_cols[pl.ds(begin, wave_part), :], split, preferred_element_type=jnp.float32
        )
        cosine, sine = cos_sin(turn)
        phase_refs[order][pl.ds(begin, wave_part), :] = cosine
        after = pl.multiple_of(waves_each + begin, wave_part)
        phase_refs[order][pl.ds(after, wave_part), :] = sine

    slopes, shifts = [], []
    for kernel in range(local_kernels):
        center = (group * local_kernels + kernel).astype(jnp.float32) * (cutoff / (RADIAL - 1))
        slope = ROOT_LOG2E / width_ref[kernel]
        slopes.append(slope * 2.0**-32)
        shifts.append(slope * center)

    def weight_part(order, origin, part):
        low = pl.multiple_of(part * row_part, row_part)
        near = pos_buf[origin] << 16
        block = (part * row_part) // BLOCK
        for near_block in range(blocks_here):
            lanes = slice(near_block * BLOCK, (near_block + 1) * BLOCK)
            total = None
            for axis in range(3):
                gap = spot_cols[axis, pl.ds(low, row_part), :] - near[axis : axis + 1, lanes]
                gap = gap.astype(jnp.float32)
                total = gap * gap if total is None else total + gap * gap
            distance = total * lax.rsqrt(jnp.maximum(total, 1.0))
            level = keep_ref[block, pl.ds(origin * blocks_here + near_block, 1), :]
            fall = level * (2.0**-64 / (cutoff * cutoff))
            smooth = jnp.maximum(level - total * fall, 0.0)
            smooth = smooth * smooth
            for kernel in range(local_kernels):
                shaped = distance * slopes[kernel] - shifts[kernel]
                weights = jnp.exp2(-(shaped * shaped)) * smooth
                weight_refs[order][
                    pl.ds(pl.multiple_of(kernel * rows + low, row_part), row_part), lanes
                ] = weights.astype(jnp.bfloat16)

    def make_latent(order, origin):
        feats = feat_buf[origin].reshape(rows, channels)
        latent_refs[order][...] = jnp.dot(
            feats, fused_w[...], preferred_element_type=jnp.float32
        ).astype(jnp.bfloat16)

    def use_part(shards, part):
        size = 2 * waves_each // PIECES
        begin = pl.ds(pl.multiple_of(part * size, size), size)
        total = factors[begin, :]
        for order, _ in shards:
            total += jnp.dot(
                phase_refs[order][begin, :], latent_refs[order][...], preferred_element_type=jnp.float32
            )
        factors[begin, :] = total
        size = local_kernels * rows // PIECES
        begin = pl.ds(pl.multiple_of(part * size, size), size)
        total = gathered[begin, :]
        for order, origin in shards:
            total += jnp.dot(
                weight_refs[order][begin, :],
                feat_buf[origin].reshape(rows, channels),
                preferred_element_type=jnp.float32,
            )
        gathered[begin, :] = total

    own_pos.wait()
    spots = turned(pos_buf[me].astype(jnp.float32))
    for axis in range(3):
        column = jnp.broadcast_to(spots[:, axis : axis + 1], (rows, BLOCK))
        spot_cols[axis] = column.astype(jnp.int32) << 16
    number = lax.broadcasted_iota(jnp.int32, (n * blocks_here, BLOCK), 0)
    for block in range(blocks_here):
        level = jnp.zeros((n * blocks_here, BLOCK), jnp.float32)
        for slot in range(NBR):
            level = jnp.where(number == nbr_ref[block, slot], (NBR * BLOCK) ** -0.25, level)
        keep_ref[block] = level
    for load in loads[:4]:
        load.wait()
    waves = turned(wave_ref[...].astype(jnp.float32))
    wave_cols[...] = jnp.concatenate(
        [waves[:, :3], waves[:, :3], jnp.zeros((waves_each, 2), jnp.float32)], axis=1
    ).astype(jnp.bfloat16)
    lengths = waves[:, :1] * waves[:, :1] + waves[:, 1:2] * waves[:, 1:2]
    lengths = lengths + waves[:, 2:3] * waves[:, 2:3]
    gain_ref[...] = jnp.exp(-lengths * rate_ref[...]) * (1.0 / math.sqrt(rows * n * K))
    mix_high = mix_ref[...].astype(jnp.bfloat16)
    mix_low = (mix_ref[...] - mix_high.astype(jnp.float32)).astype(jnp.bfloat16)
    fused_w[...] = (
        jnp.dot(latw_ref[...], mix_high, preferred_element_type=jnp.float32)
        + jnp.dot(latw_ref[...], mix_low, preferred_element_type=jnp.float32)
    ).astype(jnp.bfloat16)
    factors[...] = jnp.zeros_like(factors)
    gathered[...] = jnp.zeros_like(gathered)

    def own_part(part, carry):
        phase_part(0, me, part)
        weight_part(0, me, part)
        return carry

    lax.fori_loop(0, PIECES, own_part, 0)
    own_feat.wait()

    own_side = [(0, me)] + [(2 * r - 1, 2 * ranked(r) + side) for r in range(1, lines)]
    other_side = [(2 * r + 2 if r < lines - 1 else n - 1, 2 * ranked(r) + 1 - side) for r in range(lines)]

    def wait_forwards(shard_line, shard_side):
        for which in range(PIECES):
            forward_copy(shard_line, shard_side, which).wait_recv()

    def round_of(rank):
        made = []
        used = []
        if rank < lines:
            at_distance(rank, pass_pos)
            made.append(own_side[rank])
        pos_side_copy(pos_piece(ranked(rank - 1)), ranked(rank - 1)).wait_recv()
        made.append(other_side[rank - 1])
        if rank > 1:
            wait_forwards(ranked(rank - 1), side)
        used.append(own_side[rank - 1])
        make_latent(*used[-1])
        if rank > 1:
            wait_forwards(ranked(rank - 2), 1 - side)
            used.append(other_side[rank - 2])
            make_latent(*used[-1])

        def one(part, carry):
            if rank < lines:
                at_distance(rank, lambda shard_line, upward: pass_on(shard_line, part, upward))
                shard_line = ranked(rank)
                side_copy(
                    feat_piece(shard_line, side, part), shard_line * PIECES + part
                ).start()
            shard_line = ranked(rank - 1)
            slot = shard_line * PIECES + part
            side_copy(feat_piece(shard_line, 1 - side, part), slot).wait_recv()
            forward_copy(shard_line, 1 - side, part).start()
            use_part(used, part)
            for order, origin in made:
                phase_part(order, origin, part)
                weight_part(order, origin, part)
            if rank == 1:
                size = 2 * waves_each // PIECES
                begin = pl.ds(pl.multiple_of(part * size, size), size)
                own_turned[:, begin] = phase_refs[0][begin, :].T
            return carry

        lax.fori_loop(0, PIECES, one, 0)

    for rank in range(1, lines + 1):
        round_of(rank)
    wait_forwards(ranked(lines - 1), 1 - side)
    last = [other_side[lines - 1]]
    make_latent(*last[0])
    for part in range(PIECES):
        use_part(last, part)

    filt_buf[:waves_each] = (factors[:waves_each] * gain_ref[...]).astype(jnp.bfloat16)
    filt_buf[waves_each:] = (factors[waves_each:] * gain_ref[...]).astype(jnp.bfloat16)
    reduced = jnp.dot(
        own_turned[...], filt_buf[...], preferred_element_type=jnp.float32
    ).astype(jnp.bfloat16)
    for load in loads[4:]:
        load.wait()
    width = out_ref.shape[1]
    order = sorted(range(1, groups), key=lambda step: abs(step - groups // 2))
    for step in [*order, 0]:
        target = lax.rem(group + step, groups)
        columns = pl.ds(pl.multiple_of(target * width, width), width)
        part_sum = jnp.dot(reduced, outw_ref[:, columns], preferred_element_type=jnp.float32)
        for kernel in range(local_kernels):
            part_sum += jnp.dot(
                gathered[kernel * rows : (kernel + 1) * rows].astype(jnp.bfloat16),
                short_ref[kernel, :, columns],
                preferred_element_type=jnp.float32,
            )
        if step == 0:
            total = part_sum
        else:
            send_buf[target] = part_sum.astype(jnp.bfloat16)
            msg_copy(step).start()
    for step in order[::-1]:
        msg_copy(step).wait_recv()
        total += recv_buf[step].astype(jnp.float32)
    out_ref[...] = total.astype(out_ref.dtype)

    def finish(shard_line, carry):
        piece = pos_piece(shard_line)

        @pl.when((shard_line <= line) & can_up)
        def _():
            pos_up_copy(piece, shard_line).wait_send()

        @pl.when((shard_line >= line) & can_down)
        def _():
            pos_down_copy(piece, shard_line).wait_send()

        pos_side_copy(piece, shard_line).wait_send()
        for which in range(PIECES):
            piece = feat_piece(shard_line, side, which)
            slot = shard_line * PIECES + which

            @pl.when((shard_line <= line) & can_up)
            def _():
                up_copy(piece, slot).wait_send()

            @pl.when((shard_line >= line) & can_down)
            def _():
                down_copy(piece, slot).wait_send()

            side_copy(piece, slot).wait_send()
            forward_copy(shard_line, 1 - side, which).wait_send()

            @pl.when(shard_line != line)
            def _():
                forward_copy(shard_line, side, which).wait_send()

        return carry

    lax.fori_loop(0, lines, finish, 0)
    for step in range(1, groups):
        msg_copy(step).wait_send()


def fused(
    features,
    positions,
    neighbours,
    wavevectors,
    radial_width,
    short_weight,
    latent_weight,
    mix_weight,
    filter_rate,
    out_weight,
):
    n = lax.axis_size("atoms")
    groups = lax.axis_size("waves")
    rows, channels = features.shape
    latents = latent_weight.shape[1]
    waves_each = wavevectors.shape[1]
    local_kernels = radial_width.shape[0]
    blocks = n * rows // BLOCK
    vmem = pl.BlockSpec(memory_space=pltpu.VMEM)
    held = pl.BlockSpec(memory_space=pl.ANY)
    smem = pl.BlockSpec(memory_space=pltpu.SMEM)
    dma = pltpu.SemaphoreType.DMA
    lines = n // 2
    return pl.pallas_call(
        functools.partial(fused_kernel, n, groups),
        out_shape=jax.ShapeDtypeStruct((rows, channels // groups), jnp.bfloat16),
        in_specs=[held, held, smem, held, smem, held, held, held, held, held],
        out_specs=vmem,
        scratch_shapes=[
            pltpu.VMEM(wavevectors.shape, jnp.int32),
            pltpu.VMEM(short_weight.shape, jnp.bfloat16),
            pltpu.VMEM(latent_weight.shape, jnp.bfloat16),
            pltpu.VMEM(mix_weight.shape, jnp.float32),
            pltpu.VMEM((1, latents), jnp.float32),
            pltpu.VMEM(out_weight.shape, jnp.bfloat16),
            pltpu.VMEM((n, 2, PIECES, rows // 2 // PIECES, channels), jnp.bfloat16),
            pltpu.VMEM((n, 3, rows), jnp.int32),
            pltpu.VMEM((channels, latents), jnp.bfloat16),
            pltpu.VMEM((2 * waves_each, latents), jnp.float32),
            pltpu.VMEM((local_kernels * rows, channels), jnp.float32),
            pltpu.VMEM((waves_each, 8), jnp.bfloat16),
            pltpu.VMEM((3, rows, BLOCK), jnp.int32),
            pltpu.VMEM((rows // BLOCK, blocks, BLOCK), jnp.float32),
            pltpu.VMEM((waves_each, latents), jnp.float32),
            pltpu.VMEM((rows, 2 * waves_each), jnp.bfloat16),
            pltpu.VMEM((2 * waves_each, latents), jnp.bfloat16),
            pltpu.VMEM((groups, rows, channels // groups), jnp.bfloat16),
            pltpu.VMEM((groups, rows, channels // groups), jnp.bfloat16),
            *[pltpu.VMEM((2 * waves_each, rows), jnp.bfloat16) for _ in range(n)],
            *[pltpu.VMEM((local_kernels * rows, rows), jnp.bfloat16) for _ in range(n)],
            *[pltpu.VMEM((rows, latents), jnp.bfloat16) for _ in range(n)],
            dma((8,)),
            *[dma((lines * PIECES,)) for _ in range(5)],
            *[dma((n * PIECES,)) for _ in range(2)],
            *[dma((lines,)) for _ in range(5)],
            *[dma((groups,)) for _ in range(2)],
        ],
        compiler_params=pltpu.CompilerParams(
            collective_id=0, has_side_effects=True, vmem_limit_bytes=VMEM_LIMIT
        ),
    )(
        features.reshape(2, PIECES, rows // 2 // PIECES, channels),
        positions,
        neighbours,
        wavevectors,
        radial_width,
        short_weight,
        latent_weight,
        mix_weight,
        filter_rate.reshape(1, latents),
        out_weight,
    )


def layer(*arrays):
    features, wavevectors = arrays[0], arrays[3]
    n = lax.axis_size("atoms")
    groups = lax.axis_size("waves")
    rows = features.shape[0]
    reach_hops = -(-REACH // (rows // BLOCK))
    covers_all = 2 * reach_hops + 1 >= n
    if covers_all and groups == 4 and n % 2 == 0 and rows == 2 * BLOCK:
        if wavevectors.shape[1] % 512 == 0 and arrays[6].shape[1] % 128 == 0:
            return fused(*arrays)
    return local(*arrays)


def solution(mesh):
    placed = (
        P("atoms", None),
        P(None, "atoms"),
        P("atoms", None),
        P(None, "waves"),
        P("waves"),
        P("waves", None, None),
        P(),
        P(),
        P(),
        P(),
    )
    return jax.shard_map(
        layer, mesh=mesh, in_specs=placed, out_specs=P("atoms", "waves"), check_vma=False
    )
```

```python
import functools
import math

import jax
import jax.numpy as jnp
from jax import lax
from jax.experimental import pallas as pl
from jax.experimental.pallas import tpu as pltpu
from jax.sharding import PartitionSpec as P

K = 4096
RADIAL = 8
BLOCK = 128
NBR = 12
REACH = 7


cutoff = 0.5


def shifted(value, axis, steps):
    count = lax.axis_size(axis)
    pairs = [(source, (source + steps) % count) for source in range(count)]
    return lax.ppermute(value, axis, pairs)


def kernels(own_pos, near_pos, centers, radial_width):
    offsets = own_pos[:, None, :, None] - near_pos[:, :, None, :]
    offsets = jnp.mod(offsets, 65536)
    offsets = jnp.where(offsets >= 32768, offsets - 65536, offsets)
    coords = offsets.astype(jnp.float32) * (1.0 / 65536.0)
    dist_sq = jnp.sum(coords * coords, axis=0)
    distance = jnp.sqrt(dist_sq)
    smooth = jnp.where(
        dist_sq < cutoff * cutoff, jnp.square(1.0 - dist_sq / (cutoff * cutoff)), 0.0
    )
    shaped = (distance[None] - centers[:, None, None, None]) / radial_width[:, None, None, None]
    norm_scale = 1.0 / math.sqrt(NBR * BLOCK)
    return (jnp.exp(-jnp.square(shaped)) * smooth[None] * norm_scale).astype(jnp.bfloat16)


def phases_of(wavevectors, spots):
    phase_turn = (
        wavevectors[0][:, None] * spots[0][None, :]
        + wavevectors[1][:, None] * spots[1][None, :]
        + wavevectors[2][:, None] * spots[2][None, :]
    )
    phase_turn = jnp.mod(phase_turn, 65536)
    angles = phase_turn.astype(jnp.float32) * (2.0 * math.pi / 65536.0)
    return jnp.concatenate([jnp.cos(angles), jnp.sin(angles)], axis=0).astype(jnp.bfloat16)


def filter_gain(wavevectors, filter_rate):
    lengths = jnp.sum(wavevectors * wavevectors, axis=0).astype(jnp.float32)
    return jnp.exp(-lengths[:, None] * filter_rate[None, :])


def local(
    features,
    positions,
    neighbours,
    wavevectors,
    radial_width,
    short_weight,
    latent_weight,
    mix_weight,
    filter_rate,
    out_weight,
):
    row_count = features.shape[0]
    channels = features.shape[1]
    blocks_here = row_count // BLOCK
    atom_devices = lax.axis_size("atoms")
    total_blocks = blocks_here * atom_devices
    reach_hops = -(-REACH // blocks_here)
    window_feat = []
    window_pos = []
    for offset in range(-reach_hops, reach_hops + 1):
        if offset == 0:
            arrived = (features, positions)
        else:
            arrived = shifted((features, positions), "atoms", -offset)
        window_feat.append(arrived[0])
        window_pos.append(arrived[1])
    window_feat = jnp.concatenate(window_feat, axis=0).reshape(-1, BLOCK, channels)
    window_pos = jnp.concatenate(window_pos, axis=1).reshape(3, -1, BLOCK)
    first_block = lax.axis_index("atoms") * blocks_here - reach_hops * blocks_here
    local_near = jnp.mod(neighbours - first_block, total_blocks)
    own_pos = positions.reshape(3, blocks_here, BLOCK)
    local_kernels = radial_width.shape[0]
    kernel_ids = lax.axis_index("waves") * local_kernels + jnp.arange(
        local_kernels, dtype=jnp.int32
    )
    centers = cutoff * kernel_ids.astype(jnp.float32) / (RADIAL - 1)
    flat_weight = short_weight.reshape(local_kernels * channels, channels)

    def short_block(block_index):
        near_blocks = local_near[block_index]
        near_feat = jnp.stack(
            [lax.dynamic_index_in_dim(window_feat, near_blocks[j], 0, False) for j in range(NBR)]
        )
        near_pos = jnp.stack(
            [lax.dynamic_index_in_dim(window_pos, near_blocks[j], 1, False) for j in range(NBR)],
            axis=1,
        )
        weights = kernels(own_pos[:, block_index], near_pos, centers, radial_width)
        gathered = jnp.einsum(
            "rjia,jac->irc", weights, near_feat, preferred_element_type=jnp.float32
        )
        gathered = gathered.astype(jnp.bfloat16).reshape(BLOCK, local_kernels * channels)
        return jnp.dot(gathered, flat_weight, preferred_element_type=jnp.float32)

    short_range = lax.map(short_block, jnp.arange(blocks_here, dtype=jnp.int32)).reshape(
        row_count, channels
    )
    latent = jnp.dot(features, latent_weight, preferred_element_type=jnp.float32).astype(
        jnp.bfloat16
    )
    phases = phases_of(wavevectors, positions)
    partial_factors = jnp.dot(phases, latent, preferred_element_type=jnp.float32)
    gain = filter_gain(wavevectors, filter_rate)
    gain = jnp.concatenate([gain, gain], axis=0)
    norm_scale = 1.0 / math.sqrt(row_count * atom_devices)
    factors = lax.psum(partial_factors, "atoms")
    mixed = jnp.dot(factors, mix_weight, precision=lax.Precision.HIGHEST)
    filtered = (gain * mixed * norm_scale).astype(jnp.bfloat16)
    summed = lax.dot_general(
        phases, filtered, (((0,), (0,)), ((), ())), preferred_element_type=jnp.float32
    )
    summed = (summed * (1.0 / math.sqrt(K))).astype(jnp.bfloat16)
    long_range = jnp.dot(summed, out_weight, preferred_element_type=jnp.float32)
    combined = lax.psum_scatter(
        (short_range + long_range).astype(jnp.bfloat16), "waves", scatter_dimension=1, tiled=True
    )
    return combined


MESH = pl.DeviceIdType.MESH
PIECES = 4
VMEM_LIMIT = 67043328
HALF_SINE = (4.44153573, -7.26468112, 3.2520508)
HALF_COSINE = (1.41449234, -6.98577464, 5.77484937, -1.8561312)
ROOT_LOG2E = math.sqrt(math.log2(math.e))


def cos_sin(turn):
    turn = turn - jnp.round(turn)
    square = turn * turn
    half_sine = HALF_SINE[-1] * square + HALF_SINE[-2]
    half_sine = (half_sine * square + HALF_SINE[0]) * turn
    half_cosine = HALF_COSINE[-1] * square + HALF_COSINE[-2]
    half_cosine = half_cosine * square + HALF_COSINE[1]
    half_cosine = half_cosine * square + HALF_COSINE[0]
    return (
        (1.0 - half_sine * half_sine).astype(jnp.bfloat16),
        (half_sine * half_cosine).astype(jnp.bfloat16),
    )


def turned(rows):
    padded = jnp.concatenate([rows, jnp.zeros((5, rows.shape[1]), jnp.float32)], axis=0)
    return padded.T


def fused_kernel(
    n,
    groups,
    feat_ref,
    pos_ref,
    nbr_in,
    wave_in,
    width_in,
    short_in,
    latw_in,
    mix_in,
    rate_in,
    outw_in,
    out_ref,
    nbr_ref,
    width_ref,
    wave_ref,
    short_ref,
    latw_ref,
    mix_ref,
    rate_ref,
    outw_ref,
    feat_buf,
    pos_buf,
    fused_w,
    factors,
    gathered,
    wave_cols,
    spot_cols,
    keep_ref,
    gain_ref,
    own_turned,
    short_buf,
    send_buf,
    recv_buf,
    *rest,
):
    phase_refs, rest = rest[:n], rest[n:]
    weight_refs, rest = rest[:n], rest[n:]
    latent_refs, rest = rest[:n], rest[n:]
    (
        own_sem,
        line_up,
        line_down,
        line_recv,
        side_send,
        side_recv,
        fwd_send,
        fwd_recv,
        pos_up,
        pos_down,
        pos_line,
        pos_side_send,
        pos_side,
        msg_send,
        msg_recv,
    ) = rest
    me = lax.axis_index("atoms")
    group = lax.axis_index("waves")
    core, plane = lax.rem(group, 2), group // 2
    partner = group + 1 - 2 * core
    half, channels = feat_ref.shape[1] * feat_ref.shape[2], feat_ref.shape[3]
    rows = 2 * half
    blocks_here = rows // BLOCK
    local_kernels = short_ref.shape[0]
    waves_each = wave_ref.shape[1]
    lines = n // 2
    line, side = me // 2, lax.rem(me, 2)
    can_up, can_down = line < lines - 1, line > 0

    def ranked(rank):
        closest = jnp.minimum(line, lines - 1 - line)
        away = (rank + 1) // 2
        near_line = jnp.where(lax.rem(rank, 2) == 1, line - away, line + away)
        far_line = jnp.where(line < lines - 1 - line, rank, lines - 1 - rank)
        return jnp.where(rank <= 2 * closest, near_line, far_line)

    def remote(piece, send_sem, recv_sem, device):
        return pltpu.make_async_remote_copy(
            src_ref=piece[0],
            dst_ref=piece[1],
            send_sem=send_sem,
            recv_sem=recv_sem,
            device_id=device,
            device_id_type=MESH,
        )

    to_up, to_down = {"atoms": me + 2}, {"atoms": me - 2}
    to_side, to_core = {"atoms": me + 1 - 2 * side}, {"waves": partner}

    def feat_piece(shard_line, shard_side, which):
        place = feat_buf.at[2 * shard_line + shard_side, core, which]
        return place, place

    def own_piece(which):
        return feat_ref.at[core, which], feat_buf.at[me, core, which]

    def pos_piece(shard_line):
        place = pos_buf.at[2 * shard_line + side]
        return place, place

    own_pos_piece = (pos_ref, pos_buf.at[me])

    def up_copy(piece, slot):
        return remote(piece, line_up.at[slot], line_recv.at[slot], to_up)

    def down_copy(piece, slot):
        return remote(piece, line_down.at[slot], line_recv.at[slot], to_down)

    def side_copy(piece, slot):
        return remote(piece, side_send.at[slot], side_recv.at[slot], to_side)

    def forward_copy(shard_line, shard_side, which):
        slot = (2 * shard_line + shard_side) * PIECES + which
        return remote(
            feat_piece(shard_line, shard_side, which), fwd_send.at[slot], fwd_recv.at[slot], to_core
        )

    def pos_up_copy(piece, shard):
        return remote(piece, pos_up.at[shard], pos_line.at[shard], to_up)

    def pos_down_copy(piece, shard):
        return remote(piece, pos_down.at[shard], pos_line.at[shard], to_down)

    def pos_side_copy(piece, shard):
        return remote(piece, pos_side_send.at[shard], pos_side.at[shard], to_side)

    def msg_copy(step):
        target = lax.rem(group + step, groups)
        return remote(
            (send_buf.at[target], recv_buf.at[step]),
            msg_send.at[step],
            msg_recv.at[step],
            {"waves": target},
        )

    own_feat = pltpu.make_async_copy(feat_ref, feat_buf.at[me], own_sem.at[0])
    own_pos = pltpu.make_async_copy(pos_ref, pos_buf.at[me], own_sem.at[1])
    loads = [
        pltpu.make_async_copy(held, kept, own_sem.at[2 + which])
        for which, (held, kept) in enumerate(
            (
                (nbr_in, nbr_ref),
                (width_in, width_ref),
                (wave_in, wave_ref),
                (mix_in, mix_ref),
                (latw_in, latw_ref),
                (rate_in, rate_ref),
                (short_in, short_ref),
                (outw_in, outw_ref),
            )
        )
    ]

    barrier = pltpu.get_barrier_semaphore()

    @pl.when(can_up)
    def _():
        pl.semaphore_signal(barrier, inc=1, device_id=to_up, device_id_type=MESH)

    @pl.when(can_down)
    def _():
        pl.semaphore_signal(barrier, inc=1, device_id=to_down, device_id_type=MESH)

    pl.semaphore_signal(barrier, inc=1, device_id=to_side, device_id_type=MESH)
    for step in range(1, groups):
        pl.semaphore_signal(
            barrier,
            inc=1,
            device_id={"waves": lax.rem(group + step, groups)},
            device_id_type=MESH,
        )
    own_pos.start()
    for load in loads[:6]:
        load.start()
    own_feat.start()
    for load in loads[6:]:
        load.start()
    pl.semaphore_wait(
        barrier, groups + jnp.where(can_up, 1, 0) + jnp.where(can_down, 1, 0)
    )

    @pl.when(can_up)
    def _():
        pos_up_copy(own_pos_piece, line).start()

    @pl.when(can_down)
    def _():
        pos_down_copy(own_pos_piece, line).start()

    pos_side_copy(own_pos_piece, line).start()
    for which in range(PIECES):
        slot = line * PIECES + which

        @pl.when(can_up)
        def _():
            up_copy(own_piece(which), slot).start()

        @pl.when(can_down)
        def _():
            down_copy(own_piece(which), slot).start()

        side_copy(own_piece(which), slot).start()

    def pass_on(shard_line, which, upward):
        piece = feat_piece(shard_line, side, which)
        slot = shard_line * PIECES + which
        up_copy(piece, slot).wait_recv()
        if upward:

            @pl.when(can_up)
            def _():
                up_copy(piece, slot).start()

        else:

            @pl.when(can_down)
            def _():
                down_copy(piece, slot).start()

        side_copy(piece, slot).start()
        forward_copy(shard_line, side, which).start()

    def pass_pos(shard_line, upward):
        piece = pos_piece(shard_line)
        pos_up_copy(piece, shard_line).wait_recv()
        if upward:

            @pl.when(can_up)
            def _():
                pos_up_copy(piece, shard_line).start()

        else:

            @pl.when(can_down)
            def _():
                pos_down_copy(piece, shard_line).start()

        pos_side_copy(piece, shard_line).start()

    def at_distance(distance, act):
        @pl.when(line >= distance)
        def _():
            act(line - distance, True)

        @pl.when(line < lines - distance)
        def _():
            act(line + distance, False)

    wave_part = waves_each // PIECES
    row_part = rows // PIECES

    def phase_part(order, origin, part):
        position = pos_buf[origin]
        high = position >> 8
        low = position - (high << 8)
        split = jnp.concatenate(
            [
                high.astype(jnp.float32) * (1.0 / 256.0),
                low.astype(jnp.float32) * (1.0 / 65536.0),
                jnp.zeros((2, rows), jnp.float32),
            ],
            axis=0,
        ).astype(jnp.bfloat16)
        begin = pl.multiple_of(part * wave_part, wave_part)
        turn = jnp.dot(
            wave_cols[pl.ds(begin, wave_part), :], split, preferred_element_type=jnp.float32
        )
        cosine, sine = cos_sin(turn)
        phase_refs[order][pl.ds(begin, wave_part), :] = cosine
        after = pl.multiple_of(waves_each + begin, wave_part)
        phase_refs[order][pl.ds(after, wave_part), :] = sine

    def weight_part(order, origin, part):
        low = pl.multiple_of(part * row_part, row_part)
        near = pos_buf[origin] << 16
        block = (part * row_part) // BLOCK
        for near_block in range(blocks_here):
            lanes = slice(near_block * BLOCK, (near_block + 1) * BLOCK)
            total = None
            for axis in range(3):
                gap = spot_cols[axis, pl.ds(low, row_part), :] - near[axis : axis + 1, lanes]
                gap = gap.astype(jnp.float32)
                total = gap * gap if total is None else total + gap * gap
            distance = total * lax.rsqrt(jnp.maximum(total, 1.0))
            level = keep_ref[block, pl.ds(origin * blocks_here + near_block, 1), :]
            fall = level * (2.0**-64 / (cutoff * cutoff))
            smooth = jnp.maximum(level - total * fall, 0.0)
            smooth = smooth * smooth
            for kernel in range(local_kernels):
                shaped = distance * slopes[kernel] - shifts[kernel]
                weights = jnp.exp2(-(shaped * shaped)) * smooth
                weight_refs[order][
                    pl.ds(pl.multiple_of(kernel * rows + low, row_part), row_part), lanes
                ] = weights.astype(jnp.bfloat16)

    def make_latent(order, origin):
        feats = feat_buf[origin].reshape(rows, channels)
        latent_refs[order][...] = jnp.dot(
            feats, fused_w[...], preferred_element_type=jnp.float32
        ).astype(jnp.bfloat16)

    def use_part(shards, part):
        size = 2 * waves_each // PIECES
        begin = pl.ds(pl.multiple_of(part * size, size), size)
        total = factors[begin, :]
        for order, _ in shards:
            total += jnp.dot(
                phase_refs[order][begin, :], latent_refs[order][...], preferred_element_type=jnp.float32
            )
        factors[begin, :] = total
        size = local_kernels * rows // PIECES
        begin = pl.ds(pl.multiple_of(part * size, size), size)
        total = gathered[begin, :]
        for order, origin in shards:
            total += jnp.dot(
                weight_refs[order][begin, :],
                feat_buf[origin].reshape(rows, channels),
                preferred_element_type=jnp.float32,
            )
        gathered[begin, :] = total

    own_pos.wait()
    for load in loads[:6]:
        load.wait()
    slopes, shifts = [], []
    for kernel in range(local_kernels):
        center = (group * local_kernels + kernel).astype(jnp.float32) * (cutoff / (RADIAL - 1))
        slope = ROOT_LOG2E / width_ref[kernel]
        slopes.append(slope * 2.0**-32)
        shifts.append(slope * center)
    spots = turned(pos_buf[me].astype(jnp.float32))
    for axis in range(3):
        column = jnp.broadcast_to(spots[:, axis : axis + 1], (rows, BLOCK))
        spot_cols[axis] = column.astype(jnp.int32) << 16
    number = lax.broadcasted_iota(jnp.int32, (n * blocks_here, BLOCK), 0)
    for block in range(blocks_here):
        level = jnp.zeros((n * blocks_here, BLOCK), jnp.float32)
        for slot in range(NBR):
            level = jnp.where(number == nbr_ref[block, slot], (NBR * BLOCK) ** -0.25, level)
        keep_ref[block] = level
    waves = turned(wave_ref[...].astype(jnp.float32))
    wave_cols[...] = jnp.concatenate(
        [waves[:, :3], waves[:, :3], jnp.zeros((waves_each, 2), jnp.float32)], axis=1
    ).astype(jnp.bfloat16)
    lengths = waves[:, :1] * waves[:, :1] + waves[:, 1:2] * waves[:, 1:2]
    lengths = lengths + waves[:, 2:3] * waves[:, 2:3]
    gain_ref[...] = jnp.exp(-lengths * rate_ref[...]) * (1.0 / math.sqrt(rows * n * K))
    mix_high = mix_ref[...].astype(jnp.bfloat16)
    mix_low = (mix_ref[...] - mix_high.astype(jnp.float32)).astype(jnp.bfloat16)
    fused_w[...] = (
        jnp.dot(latw_ref[...], mix_high, preferred_element_type=jnp.float32)
        + jnp.dot(latw_ref[...], mix_low, preferred_element_type=jnp.float32)
    ).astype(jnp.bfloat16)
    factors[...] = jnp.zeros_like(factors)
    gathered[...] = jnp.zeros_like(gathered)

    def own_part(part, carry):
        phase_part(0, me, part)
        weight_part(0, me, part)
        return carry

    lax.fori_loop(0, PIECES, own_part, 0)
    own_feat.wait()

    own_side = [(0, me)] + [(2 * r - 1, 2 * ranked(r) + side) for r in range(1, lines)]
    other_side = [(2 * r + 2 if r < lines - 1 else n - 1, 2 * ranked(r) + 1 - side) for r in range(lines)]

    def wait_forwards(shard_line, shard_side):
        for which in range(PIECES):
            forward_copy(shard_line, shard_side, which).wait_recv()

    def round_of(rank):
        made = []
        used = []
        if rank < lines:
            at_distance(rank, pass_pos)
            made.append(own_side[rank])
        pos_side_copy(pos_piece(ranked(rank - 1)), ranked(rank - 1)).wait_recv()
        made.append(other_side[rank - 1])
        used.append(own_side[rank - 1])
        if rank > 1:
            used.append(other_side[rank - 2])

        def one(part, carry):
            if rank < lines:
                at_distance(rank, lambda shard_line, upward: pass_on(shard_line, part, upward))
            shard_line = ranked(rank - 1)
            slot = shard_line * PIECES + part
            side_copy(feat_piece(shard_line, 1 - side, part), slot).wait_recv()
            forward_copy(shard_line, 1 - side, part).start()

            @pl.when(part == 0)
            def _():
                if rank > 1:
                    wait_forwards(ranked(rank - 1), side)
                    wait_forwards(ranked(rank - 2), 1 - side)
                for held in used:
                    make_latent(*held)

            use_part(used, part)
            for order, origin in made:
                phase_part(order, origin, part)
                weight_part(order, origin, part)
            if rank == 1:
                size = 2 * waves_each // PIECES
                begin = pl.ds(pl.multiple_of(part * size, size), size)
                own_turned[:, begin] = phase_refs[0][begin, :].T
            return carry

        lax.fori_loop(0, PIECES, one, 0)

    for rank in range(1, lines + 1):
        round_of(rank)
    wait_forwards(ranked(lines - 1), 1 - side)
    order, origin = other_side[lines - 1]
    make_latent(order, origin)
    size = waves_each // 2
    reduced = jnp.zeros((rows, gain_ref.shape[1]), jnp.float32)
    for part in range(4):
        begin = slice(part * size, (part + 1) * size)
        total = factors[begin, :] + jnp.dot(
            phase_refs[order][begin, :], latent_refs[order][...], preferred_element_type=jnp.float32
        )
        low = (part % 2) * size
        filtered = (total * gain_ref[low : low + size, :]).astype(jnp.bfloat16)
        reduced += jnp.dot(own_turned[:, begin], filtered, preferred_element_type=jnp.float32)
    reduced = reduced.astype(jnp.bfloat16)
    size = local_kernels * rows // PIECES
    for part in range(PIECES):
        begin = slice(part * size, (part + 1) * size)
        total = gathered[begin, :] + jnp.dot(
            weight_refs[order][begin, :],
            feat_buf[origin].reshape(rows, channels),
            preferred_element_type=jnp.float32,
        )
        short_buf[begin, :] = total.astype(jnp.bfloat16)
    for load in loads[6:]:
        load.wait()
    width = out_ref.shape[1]

    def part_sum(chip):
        columns = pl.ds(pl.multiple_of(chip * 2 * width, 2 * width), 2 * width)
        total = jnp.dot(reduced, outw_ref[:, columns], preferred_element_type=jnp.float32)
        for kernel in range(local_kernels):
            total += jnp.dot(
                short_buf[kernel * rows : (kernel + 1) * rows],
                short_ref[kernel, :, columns],
                preferred_element_type=jnp.float32,
            )
        return total

    far = part_sum(1 - plane)
    left, right = far[:, :width], far[:, width:]
    send_buf[2 * (1 - plane) + core] = jnp.where(core == 0, left, right).astype(jnp.bfloat16)
    msg_copy(2).start()
    send_buf[2 * (1 - plane) + 1 - core] = jnp.where(core == 0, right, left).astype(jnp.bfloat16)
    msg_copy(3 - 2 * core).start()
    near = part_sum(plane)
    first, second = near[:, :width], near[:, width:]
    send_buf[partner] = jnp.where(core == 0, second, first).astype(jnp.bfloat16)
    msg_copy(1 + 2 * core).start()
    total = jnp.where(core == 0, first, second)
    for step in range(1, groups):
        msg_copy(step).wait_recv()
        total += recv_buf[step].astype(jnp.float32)
    out_ref[...] = total.astype(out_ref.dtype)

    def finish(shard_line, carry):
        piece = pos_piece(shard_line)

        @pl.when((shard_line <= line) & can_up)
        def _():
            pos_up_copy(piece, shard_line).wait_send()

        @pl.when((shard_line >= line) & can_down)
        def _():
            pos_down_copy(piece, shard_line).wait_send()

        pos_side_copy(piece, shard_line).wait_send()
        for which in range(PIECES):
            piece = feat_piece(shard_line, side, which)
            slot = shard_line * PIECES + which

            @pl.when((shard_line <= line) & can_up)
            def _():
                up_copy(piece, slot).wait_send()

            @pl.when((shard_line >= line) & can_down)
            def _():
                down_copy(piece, slot).wait_send()

            side_copy(piece, slot).wait_send()
            forward_copy(shard_line, 1 - side, which).wait_send()

            @pl.when(shard_line != line)
            def _():
                forward_copy(shard_line, side, which).wait_send()

        return carry

    lax.fori_loop(0, lines, finish, 0)
    for step in range(1, groups):
        msg_copy(step).wait_send()


def fused(
    features,
    positions,
    neighbours,
    wavevectors,
    radial_width,
    short_weight,
    latent_weight,
    mix_weight,
    filter_rate,
    out_weight,
):
    n = lax.axis_size("atoms")
    groups = lax.axis_size("waves")
    rows, channels = features.shape
    latents = latent_weight.shape[1]
    waves_each = wavevectors.shape[1]
    local_kernels = radial_width.shape[0]
    blocks = n * rows // BLOCK
    vmem = pl.BlockSpec(memory_space=pltpu.VMEM)
    held = pl.BlockSpec(memory_space=pl.ANY)
    dma = pltpu.SemaphoreType.DMA
    lines = n // 2
    return pl.pallas_call(
        functools.partial(fused_kernel, n, groups),
        out_shape=jax.ShapeDtypeStruct((rows, channels // groups), jnp.bfloat16),
        in_specs=[held] * 10,
        out_specs=vmem,
        scratch_shapes=[
            pltpu.SMEM(neighbours.shape, jnp.int32),
            pltpu.SMEM(radial_width.shape, jnp.float32),
            pltpu.VMEM(wavevectors.shape, jnp.int32),
            pltpu.VMEM(short_weight.shape, jnp.bfloat16),
            pltpu.VMEM(latent_weight.shape, jnp.bfloat16),
            pltpu.VMEM(mix_weight.shape, jnp.float32),
            pltpu.VMEM((1, latents), jnp.float32),
            pltpu.VMEM(out_weight.shape, jnp.bfloat16),
            pltpu.VMEM((n, 2, PIECES, rows // 2 // PIECES, channels), jnp.bfloat16),
            pltpu.VMEM((n, 3, rows), jnp.int32),
            pltpu.VMEM((channels, latents), jnp.bfloat16),
            pltpu.VMEM((2 * waves_each, latents), jnp.float32),
            pltpu.VMEM((local_kernels * rows, channels), jnp.float32),
            pltpu.VMEM((waves_each, 8), jnp.bfloat16),
            pltpu.VMEM((3, rows, BLOCK), jnp.int32),
            pltpu.VMEM((rows // BLOCK, blocks, BLOCK), jnp.float32),
            pltpu.VMEM((waves_each, latents), jnp.float32),
            pltpu.VMEM((rows, 2 * waves_each), jnp.bfloat16),
            pltpu.VMEM((local_kernels * rows, channels), jnp.bfloat16),
            pltpu.VMEM((groups, rows, channels // groups), jnp.bfloat16),
            pltpu.VMEM((groups, rows, channels // groups), jnp.bfloat16),
            *[pltpu.VMEM((2 * waves_each, rows), jnp.bfloat16) for _ in range(n)],
            *[pltpu.VMEM((local_kernels * rows, rows), jnp.bfloat16) for _ in range(n)],
            *[pltpu.VMEM((rows, latents), jnp.bfloat16) for _ in range(n)],
            dma((10,)),
            *[dma((lines * PIECES,)) for _ in range(5)],
            *[dma((n * PIECES,)) for _ in range(2)],
            *[dma((lines,)) for _ in range(5)],
            *[dma((groups,)) for _ in range(2)],
        ],
        compiler_params=pltpu.CompilerParams(
            collective_id=0, has_side_effects=True, vmem_limit_bytes=VMEM_LIMIT
        ),
    )(
        features.reshape(2, PIECES, rows // 2 // PIECES, channels),
        positions,
        neighbours,
        wavevectors,
        radial_width,
        short_weight,
        latent_weight,
        mix_weight,
        filter_rate.reshape(1, latents),
        out_weight,
    )


def layer(*arrays):
    features, wavevectors = arrays[0], arrays[3]
    n = lax.axis_size("atoms")
    groups = lax.axis_size("waves")
    rows = features.shape[0]
    reach_hops = -(-REACH // (rows // BLOCK))
    covers_all = 2 * reach_hops + 1 >= n
    if covers_all and groups == 4 and n % 2 == 0 and rows == 2 * BLOCK:
        if wavevectors.shape[1] % 512 == 0 and arrays[6].shape[1] % 128 == 0:
            return fused(*arrays)
    return local(*arrays)


def solution(mesh):
    placed = (
        P("atoms", None),
        P(None, "atoms"),
        P("atoms", None),
        P(None, "waves"),
        P("waves"),
        P("waves", None, None),
        P(),
        P(),
        P(),
        P(),
    )
    return jax.shard_map(
        layer, mesh=mesh, in_specs=placed, out_specs=P("atoms", "waves"), check_vma=False
    )
```

```python
import functools
import math

import jax
import jax.numpy as jnp
from jax import lax
from jax.experimental import pallas as pl
from jax.experimental.pallas import tpu as pltpu
from jax.sharding import PartitionSpec as P

K = 4096
RADIAL = 8
BLOCK = 128
NBR = 12
REACH = 7


cutoff = 0.5


def shifted(value, axis, steps):
    count = lax.axis_size(axis)
    pairs = [(source, (source + steps) % count) for source in range(count)]
    return lax.ppermute(value, axis, pairs)


def kernels(own_pos, near_pos, centers, radial_width):
    offsets = own_pos[:, None, :, None] - near_pos[:, :, None, :]
    offsets = jnp.mod(offsets, 65536)
    offsets = jnp.where(offsets >= 32768, offsets - 65536, offsets)
    coords = offsets.astype(jnp.float32) * (1.0 / 65536.0)
    dist_sq = jnp.sum(coords * coords, axis=0)
    distance = jnp.sqrt(dist_sq)
    smooth = jnp.where(
        dist_sq < cutoff * cutoff, jnp.square(1.0 - dist_sq / (cutoff * cutoff)), 0.0
    )
    shaped = (distance[None] - centers[:, None, None, None]) / radial_width[:, None, None, None]
    norm_scale = 1.0 / math.sqrt(NBR * BLOCK)
    return (jnp.exp(-jnp.square(shaped)) * smooth[None] * norm_scale).astype(jnp.bfloat16)


def phases_of(wavevectors, spots):
    phase_turn = (
        wavevectors[0][:, None] * spots[0][None, :]
        + wavevectors[1][:, None] * spots[1][None, :]
        + wavevectors[2][:, None] * spots[2][None, :]
    )
    phase_turn = jnp.mod(phase_turn, 65536)
    angles = phase_turn.astype(jnp.float32) * (2.0 * math.pi / 65536.0)
    return jnp.concatenate([jnp.cos(angles), jnp.sin(angles)], axis=0).astype(jnp.bfloat16)


def filter_gain(wavevectors, filter_rate):
    lengths = jnp.sum(wavevectors * wavevectors, axis=0).astype(jnp.float32)
    return jnp.exp(-lengths[:, None] * filter_rate[None, :])


def local(
    features,
    positions,
    neighbours,
    wavevectors,
    radial_width,
    short_weight,
    latent_weight,
    mix_weight,
    filter_rate,
    out_weight,
):
    row_count = features.shape[0]
    channels = features.shape[1]
    blocks_here = row_count // BLOCK
    atom_devices = lax.axis_size("atoms")
    total_blocks = blocks_here * atom_devices
    reach_hops = -(-REACH // blocks_here)
    window_feat = []
    window_pos = []
    for offset in range(-reach_hops, reach_hops + 1):
        if offset == 0:
            arrived = (features, positions)
        else:
            arrived = shifted((features, positions), "atoms", -offset)
        window_feat.append(arrived[0])
        window_pos.append(arrived[1])
    window_feat = jnp.concatenate(window_feat, axis=0).reshape(-1, BLOCK, channels)
    window_pos = jnp.concatenate(window_pos, axis=1).reshape(3, -1, BLOCK)
    first_block = lax.axis_index("atoms") * blocks_here - reach_hops * blocks_here
    local_near = jnp.mod(neighbours - first_block, total_blocks)
    own_pos = positions.reshape(3, blocks_here, BLOCK)
    local_kernels = radial_width.shape[0]
    kernel_ids = lax.axis_index("waves") * local_kernels + jnp.arange(
        local_kernels, dtype=jnp.int32
    )
    centers = cutoff * kernel_ids.astype(jnp.float32) / (RADIAL - 1)
    flat_weight = short_weight.reshape(local_kernels * channels, channels)

    def short_block(block_index):
        near_blocks = local_near[block_index]
        near_feat = jnp.stack(
            [lax.dynamic_index_in_dim(window_feat, near_blocks[j], 0, False) for j in range(NBR)]
        )
        near_pos = jnp.stack(
            [lax.dynamic_index_in_dim(window_pos, near_blocks[j], 1, False) for j in range(NBR)],
            axis=1,
        )
        weights = kernels(own_pos[:, block_index], near_pos, centers, radial_width)
        gathered = jnp.einsum(
            "rjia,jac->irc", weights, near_feat, preferred_element_type=jnp.float32
        )
        gathered = gathered.astype(jnp.bfloat16).reshape(BLOCK, local_kernels * channels)
        return jnp.dot(gathered, flat_weight, preferred_element_type=jnp.float32)

    short_range = lax.map(short_block, jnp.arange(blocks_here, dtype=jnp.int32)).reshape(
        row_count, channels
    )
    latent = jnp.dot(features, latent_weight, preferred_element_type=jnp.float32).astype(
        jnp.bfloat16
    )
    phases = phases_of(wavevectors, positions)
    partial_factors = jnp.dot(phases, latent, preferred_element_type=jnp.float32)
    gain = filter_gain(wavevectors, filter_rate)
    gain = jnp.concatenate([gain, gain], axis=0)
    norm_scale = 1.0 / math.sqrt(row_count * atom_devices)
    factors = lax.psum(partial_factors, "atoms")
    mixed = jnp.dot(factors, mix_weight, precision=lax.Precision.HIGHEST)
    filtered = (gain * mixed * norm_scale).astype(jnp.bfloat16)
    summed = lax.dot_general(
        phases, filtered, (((0,), (0,)), ((), ())), preferred_element_type=jnp.float32
    )
    summed = (summed * (1.0 / math.sqrt(K))).astype(jnp.bfloat16)
    long_range = jnp.dot(summed, out_weight, preferred_element_type=jnp.float32)
    combined = lax.psum_scatter(
        (short_range + long_range).astype(jnp.bfloat16), "waves", scatter_dimension=1, tiled=True
    )
    return combined


MESH = pl.DeviceIdType.MESH
PIECES = 4
VMEM_LIMIT = 67043328
HALF_SINE = (4.44526848, -7.31246730, 3.38876157)
HALF_COSINE = (1.41092230, -6.88237066, 4.96307940)
ROOT_LOG2E = math.sqrt(math.log2(math.e))


def cos_sin(turn):
    turn = turn - jnp.round(turn)
    square = turn * turn
    half_sine = HALF_SINE[-1] * square + HALF_SINE[-2]
    half_sine = (half_sine * square + HALF_SINE[0]) * turn
    half_cosine = HALF_COSINE[-1] * square + HALF_COSINE[-2]
    half_cosine = half_cosine * square + HALF_COSINE[0]
    return (
        (1.0 - half_sine * half_sine).astype(jnp.bfloat16),
        (half_sine * half_cosine).astype(jnp.bfloat16),
    )


def turned(rows):
    padded = jnp.concatenate([rows, jnp.zeros((5, rows.shape[1]), jnp.float32)], axis=0)
    return padded.T


def fused_kernel(
    n,
    groups,
    feat_ref,
    pos_ref,
    nbr_in,
    wave_in,
    width_in,
    short_in,
    latw_in,
    mix_in,
    rate_in,
    outw_in,
    out_ref,
    nbr_ref,
    width_ref,
    wave_ref,
    short_ref,
    latw_ref,
    mix_ref,
    rate_ref,
    outw_ref,
    feat_buf,
    pos_buf,
    fused_w,
    factors,
    gathered,
    wave_cols,
    spot_cols,
    keep_ref,
    gain_ref,
    own_turned,
    short_buf,
    send_buf,
    recv_buf,
    *rest,
):
    phase_refs, rest = rest[:n], rest[n:]
    weight_refs, rest = rest[:n], rest[n:]
    latent_refs, rest = rest[:n], rest[n:]
    (
        own_sem,
        line_up,
        line_down,
        line_recv,
        side_send,
        side_recv,
        fwd_send,
        fwd_recv,
        pos_up,
        pos_down,
        pos_line,
        pos_side_send,
        pos_side,
        msg_send,
        msg_recv,
    ) = rest
    me = lax.axis_index("atoms")
    group = lax.axis_index("waves")
    core, plane = lax.rem(group, 2), group // 2
    partner = group + 1 - 2 * core
    half, channels = feat_ref.shape[1] * feat_ref.shape[2], feat_ref.shape[3]
    rows = 2 * half
    blocks_here = rows // BLOCK
    local_kernels = short_ref.shape[0]
    waves_each = wave_ref.shape[1]
    lines = n // 2
    line, side = me // 2, lax.rem(me, 2)
    can_up, can_down = line < lines - 1, line > 0

    def ranked(rank):
        closest = jnp.minimum(line, lines - 1 - line)
        away = (rank + 1) // 2
        near_line = jnp.where(lax.rem(rank, 2) == 1, line - away, line + away)
        far_line = jnp.where(line < lines - 1 - line, rank, lines - 1 - rank)
        return jnp.where(rank <= 2 * closest, near_line, far_line)

    def remote(piece, send_sem, recv_sem, device):
        return pltpu.make_async_remote_copy(
            src_ref=piece[0],
            dst_ref=piece[1],
            send_sem=send_sem,
            recv_sem=recv_sem,
            device_id=device,
            device_id_type=MESH,
        )

    to_up, to_down = {"atoms": me + 2}, {"atoms": me - 2}
    to_side, to_core = {"atoms": me + 1 - 2 * side}, {"waves": partner}

    def feat_piece(shard_line, shard_side, which):
        place = feat_buf.at[2 * shard_line + shard_side, core, which]
        return place, place

    def own_piece(which):
        return feat_ref.at[core, which], feat_buf.at[me, core, which]

    def pos_piece(shard_line):
        place = pos_buf.at[2 * shard_line + side]
        return place, place

    own_pos_piece = (pos_ref, pos_buf.at[me])

    def up_copy(piece, slot):
        return remote(piece, line_up.at[slot], line_recv.at[slot], to_up)

    def down_copy(piece, slot):
        return remote(piece, line_down.at[slot], line_recv.at[slot], to_down)

    def side_copy(piece, slot):
        return remote(piece, side_send.at[slot], side_recv.at[slot], to_side)

    def forward_copy(shard_line, shard_side, which):
        slot = (2 * shard_line + shard_side) * PIECES + which
        return remote(
            feat_piece(shard_line, shard_side, which), fwd_send.at[slot], fwd_recv.at[slot], to_core
        )

    def pos_up_copy(piece, shard):
        return remote(piece, pos_up.at[shard], pos_line.at[shard], to_up)

    def pos_down_copy(piece, shard):
        return remote(piece, pos_down.at[shard], pos_line.at[shard], to_down)

    def pos_side_copy(piece, shard):
        return remote(piece, pos_side_send.at[shard], pos_side.at[shard], to_side)

    def msg_copy(step):
        target = lax.rem(group + step, groups)
        return remote(
            (send_buf.at[target], recv_buf.at[step]),
            msg_send.at[step],
            msg_recv.at[step],
            {"waves": target},
        )

    own_feat = pltpu.make_async_copy(feat_ref, feat_buf.at[me], own_sem.at[0])
    own_pos = pltpu.make_async_copy(pos_ref, pos_buf.at[me], own_sem.at[1])
    loads = [
        pltpu.make_async_copy(held, kept, own_sem.at[2 + which])
        for which, (held, kept) in enumerate(
            (
                (nbr_in, nbr_ref),
                (width_in, width_ref),
                (wave_in, wave_ref),
                (mix_in, mix_ref),
                (latw_in, latw_ref),
                (rate_in, rate_ref),
                (short_in, short_ref),
                (outw_in, outw_ref),
            )
        )
    ]

    barrier = pltpu.get_barrier_semaphore()

    @pl.when(can_up)
    def _():
        pl.semaphore_signal(barrier, inc=1, device_id=to_up, device_id_type=MESH)

    @pl.when(can_down)
    def _():
        pl.semaphore_signal(barrier, inc=1, device_id=to_down, device_id_type=MESH)

    pl.semaphore_signal(barrier, inc=1, device_id=to_side, device_id_type=MESH)
    for step in range(1, groups):
        pl.semaphore_signal(
            barrier,
            inc=1,
            device_id={"waves": lax.rem(group + step, groups)},
            device_id_type=MESH,
        )
    own_pos.start()
    for load in loads[:6]:
        load.start()
    own_feat.start()
    for load in loads[6:]:
        load.start()
    pl.semaphore_wait(
        barrier, groups + jnp.where(can_up, 1, 0) + jnp.where(can_down, 1, 0)
    )

    @pl.when(can_up)
    def _():
        pos_up_copy(own_pos_piece, line).start()

    @pl.when(can_down)
    def _():
        pos_down_copy(own_pos_piece, line).start()

    pos_side_copy(own_pos_piece, line).start()
    for which in range(PIECES):
        slot = line * PIECES + which

        @pl.when(can_up)
        def _():
            up_copy(own_piece(which), slot).start()

        @pl.when(can_down)
        def _():
            down_copy(own_piece(which), slot).start()

        side_copy(own_piece(which), slot).start()

    def pass_on(shard_line, which, upward):
        piece = feat_piece(shard_line, side, which)
        slot = shard_line * PIECES + which
        up_copy(piece, slot).wait_recv()
        if upward:

            @pl.when(can_up)
            def _():
                up_copy(piece, slot).start()

        else:

            @pl.when(can_down)
            def _():
                down_copy(piece, slot).start()

        side_copy(piece, slot).start()
        forward_copy(shard_line, side, which).start()

    def pass_pos(shard_line, upward):
        piece = pos_piece(shard_line)
        pos_up_copy(piece, shard_line).wait_recv()
        if upward:

            @pl.when(can_up)
            def _():
                pos_up_copy(piece, shard_line).start()

        else:

            @pl.when(can_down)
            def _():
                pos_down_copy(piece, shard_line).start()

        pos_side_copy(piece, shard_line).start()

    def at_distance(distance, act):
        @pl.when(line >= distance)
        def _():
            act(line - distance, True)

        @pl.when(line < lines - distance)
        def _():
            act(line + distance, False)

    wave_part = waves_each // PIECES
    row_part = rows // PIECES

    def phase_part(order, origin, part):
        position = pos_buf[origin]
        high = position >> 8
        low = position - (high << 8)
        split = jnp.concatenate(
            [
                high.astype(jnp.float32) * (1.0 / 256.0),
                low.astype(jnp.float32) * (1.0 / 65536.0),
                jnp.zeros((2, rows), jnp.float32),
            ],
            axis=0,
        ).astype(jnp.bfloat16)
        begin = pl.multiple_of(part * wave_part, wave_part)
        turn = jnp.dot(
            wave_cols[pl.ds(begin, wave_part), :], split, preferred_element_type=jnp.float32
        )
        cosine, sine = cos_sin(turn)
        phase_refs[order][pl.ds(begin, wave_part), :] = cosine
        after = pl.multiple_of(waves_each + begin, wave_part)
        phase_refs[order][pl.ds(after, wave_part), :] = sine

    def weight_part(order, origin, part):
        low = pl.multiple_of(part * row_part, row_part)
        near = pos_buf[origin] << 16
        block = (part * row_part) // BLOCK
        for near_block in range(blocks_here):
            lanes = slice(near_block * BLOCK, (near_block + 1) * BLOCK)
            total = None
            for axis in range(3):
                gap = spot_cols[axis, pl.ds(low, row_part), :] - near[axis : axis + 1, lanes]
                gap = gap.astype(jnp.float32)
                total = gap * gap if total is None else total + gap * gap
            distance = total * lax.rsqrt(jnp.maximum(total, 1.0))
            level = keep_ref[block, pl.ds(origin * blocks_here + near_block, 1), :]
            fall = level * (2.0**-64 / (cutoff * cutoff))
            smooth = jnp.maximum(level - total * fall, 0.0)
            smooth = smooth * smooth
            for kernel in range(local_kernels):
                shaped = distance * slopes[kernel] - shifts[kernel]
                weights = jnp.exp2(-(shaped * shaped)) * smooth
                weight_refs[order][
                    pl.ds(pl.multiple_of(kernel * rows + low, row_part), row_part), lanes
                ] = weights.astype(jnp.bfloat16)

    def make_latent(order, origin):
        feats = feat_buf[origin].reshape(rows, channels)
        latent_refs[order][...] = jnp.dot(
            feats, fused_w[...], preferred_element_type=jnp.float32
        ).astype(jnp.bfloat16)

    def use_part(shards, part):
        size = 2 * waves_each // PIECES
        begin = pl.ds(pl.multiple_of(part * size, size), size)
        total = factors[begin, :]
        for order, _ in shards:
            total += jnp.dot(
                phase_refs[order][begin, :], latent_refs[order][...], preferred_element_type=jnp.float32
            )
        factors[begin, :] = total
        size = local_kernels * rows // PIECES
        begin = pl.ds(pl.multiple_of(part * size, size), size)
        total = gathered[begin, :]
        for order, origin in shards:
            total += jnp.dot(
                weight_refs[order][begin, :],
                feat_buf[origin].reshape(rows, channels),
                preferred_element_type=jnp.float32,
            )
        gathered[begin, :] = total

    own_pos.wait()
    for load in loads[:6]:
        load.wait()
    slopes, shifts = [], []
    for kernel in range(local_kernels):
        center = (group * local_kernels + kernel).astype(jnp.float32) * (cutoff / (RADIAL - 1))
        slope = ROOT_LOG2E / width_ref[kernel]
        slopes.append(slope * 2.0**-32)
        shifts.append(slope * center)
    spots = turned(pos_buf[me].astype(jnp.float32))
    for axis in range(3):
        column = jnp.broadcast_to(spots[:, axis : axis + 1], (rows, BLOCK))
        spot_cols[axis] = column.astype(jnp.int32) << 16
    number = lax.broadcasted_iota(jnp.int32, (n * blocks_here, BLOCK), 0)
    for block in range(blocks_here):
        level = jnp.zeros((n * blocks_here, BLOCK), jnp.float32)
        for slot in range(NBR):
            level = jnp.where(number == nbr_ref[block, slot], (NBR * BLOCK) ** -0.25, level)
        keep_ref[block] = level
    waves = turned(wave_ref[...].astype(jnp.float32))
    wave_cols[...] = jnp.concatenate(
        [waves[:, :3], waves[:, :3], jnp.zeros((waves_each, 2), jnp.float32)], axis=1
    ).astype(jnp.bfloat16)
    lengths = waves[:, :1] * waves[:, :1] + waves[:, 1:2] * waves[:, 1:2]
    lengths = lengths + waves[:, 2:3] * waves[:, 2:3]
    gain_ref[...] = jnp.exp(-lengths * rate_ref[...]) * (1.0 / math.sqrt(rows * n * K))
    mix_high = mix_ref[...].astype(jnp.bfloat16)
    mix_low = (mix_ref[...] - mix_high.astype(jnp.float32)).astype(jnp.bfloat16)
    fused_w[...] = (
        jnp.dot(latw_ref[...], mix_high, preferred_element_type=jnp.float32)
        + jnp.dot(latw_ref[...], mix_low, preferred_element_type=jnp.float32)
    ).astype(jnp.bfloat16)
    factors[...] = jnp.zeros_like(factors)
    gathered[...] = jnp.zeros_like(gathered)

    def own_part(part, carry):
        phase_part(0, me, part)
        weight_part(0, me, part)
        return carry

    lax.fori_loop(0, PIECES, own_part, 0)
    own_feat.wait()

    own_side = [(0, me)] + [(2 * r - 1, 2 * ranked(r) + side) for r in range(1, lines)]
    other_side = [(2 * r + 2 if r < lines - 1 else n - 1, 2 * ranked(r) + 1 - side) for r in range(lines)]

    def wait_forwards(shard_line, shard_side):
        for which in range(PIECES):
            forward_copy(shard_line, shard_side, which).wait_recv()

    def round_of(rank):
        made = []
        used = []
        if rank < lines:
            at_distance(rank, pass_pos)
            made.append(own_side[rank])
        pos_side_copy(pos_piece(ranked(rank - 1)), ranked(rank - 1)).wait_recv()
        made.append(other_side[rank - 1])
        used.append(own_side[rank - 1])
        if rank > 1:
            used.append(other_side[rank - 2])

        def one(part, carry):
            if rank < lines:
                at_distance(rank, lambda shard_line, upward: pass_on(shard_line, part, upward))
            shard_line = ranked(rank - 1)
            slot = shard_line * PIECES + part
            side_copy(feat_piece(shard_line, 1 - side, part), slot).wait_recv()
            forward_copy(shard_line, 1 - side, part).start()

            @pl.when(part == 0)
            def _():
                if rank > 1:
                    wait_forwards(ranked(rank - 1), side)
                    wait_forwards(ranked(rank - 2), 1 - side)
                for held in used:
                    make_latent(*held)

            use_part(used, part)
            for order, origin in made:
                phase_part(order, origin, part)
                weight_part(order, origin, part)
            if rank == 1:
                size = 2 * waves_each // PIECES
                begin = pl.ds(pl.multiple_of(part * size, size), size)
                own_turned[:, begin] = phase_refs[0][begin, :].T
            return carry

        lax.fori_loop(0, PIECES, one, 0)

    for rank in range(1, lines + 1):
        round_of(rank)
    wait_forwards(ranked(lines - 1), 1 - side)
    order, origin = other_side[lines - 1]
    make_latent(order, origin)
    size = waves_each // 2
    reduced = jnp.zeros((rows, gain_ref.shape[1]), jnp.float32)
    for part in range(4):
        begin = slice(part * size, (part + 1) * size)
        total = factors[begin, :] + jnp.dot(
            phase_refs[order][begin, :], latent_refs[order][...], preferred_element_type=jnp.float32
        )
        low = (part % 2) * size
        filtered = (total * gain_ref[low : low + size, :]).astype(jnp.bfloat16)
        reduced += jnp.dot(own_turned[:, begin], filtered, preferred_element_type=jnp.float32)
    reduced = reduced.astype(jnp.bfloat16)
    size = local_kernels * rows // PIECES
    for part in range(PIECES):
        begin = slice(part * size, (part + 1) * size)
        total = gathered[begin, :] + jnp.dot(
            weight_refs[order][begin, :],
            feat_buf[origin].reshape(rows, channels),
            preferred_element_type=jnp.float32,
        )
        short_buf[begin, :] = total.astype(jnp.bfloat16)
    for load in loads[6:]:
        load.wait()
    width = out_ref.shape[1]

    def part_sum(chip):
        columns = pl.ds(pl.multiple_of(chip * 2 * width, 2 * width), 2 * width)
        total = jnp.dot(reduced, outw_ref[:, columns], preferred_element_type=jnp.float32)
        for kernel in range(local_kernels):
            total += jnp.dot(
                short_buf[kernel * rows : (kernel + 1) * rows],
                short_ref[kernel, :, columns],
                preferred_element_type=jnp.float32,
            )
        return total

    far = part_sum(1 - plane)
    left, right = far[:, :width], far[:, width:]
    send_buf[2 * (1 - plane) + core] = jnp.where(core == 0, left, right).astype(jnp.bfloat16)
    msg_copy(2).start()
    send_buf[2 * (1 - plane) + 1 - core] = jnp.where(core == 0, right, left).astype(jnp.bfloat16)
    msg_copy(3 - 2 * core).start()
    near = part_sum(plane)
    first, second = near[:, :width], near[:, width:]
    send_buf[partner] = jnp.where(core == 0, second, first).astype(jnp.bfloat16)
    msg_copy(1 + 2 * core).start()
    total = jnp.where(core == 0, first, second)
    def finish(shard_line, carry):
        piece = pos_piece(shard_line)

        @pl.when((shard_line <= line) & can_up)
        def _():
            pos_up_copy(piece, shard_line).wait_send()

        @pl.when((shard_line >= line) & can_down)
        def _():
            pos_down_copy(piece, shard_line).wait_send()

        pos_side_copy(piece, shard_line).wait_send()
        for which in range(PIECES):
            piece = feat_piece(shard_line, side, which)
            slot = shard_line * PIECES + which

            @pl.when((shard_line <= line) & can_up)
            def _():
                up_copy(piece, slot).wait_send()

            @pl.when((shard_line >= line) & can_down)
            def _():
                down_copy(piece, slot).wait_send()

            side_copy(piece, slot).wait_send()
            forward_copy(shard_line, 1 - side, which).wait_send()

            @pl.when(shard_line != line)
            def _():
                forward_copy(shard_line, side, which).wait_send()

        return carry

    lax.fori_loop(0, lines, finish, 0)
    for step in range(1, groups):
        msg_copy(step).wait_recv()
        total += recv_buf[step].astype(jnp.float32)
    out_ref[...] = total.astype(out_ref.dtype)

    for step in range(1, groups):
        msg_copy(step).wait_send()


def fused(
    features,
    positions,
    neighbours,
    wavevectors,
    radial_width,
    short_weight,
    latent_weight,
    mix_weight,
    filter_rate,
    out_weight,
):
    n = lax.axis_size("atoms")
    groups = lax.axis_size("waves")
    rows, channels = features.shape
    latents = latent_weight.shape[1]
    waves_each = wavevectors.shape[1]
    local_kernels = radial_width.shape[0]
    blocks = n * rows // BLOCK
    vmem = pl.BlockSpec(memory_space=pltpu.VMEM)
    held = pl.BlockSpec(memory_space=pl.ANY)
    dma = pltpu.SemaphoreType.DMA
    lines = n // 2
    return pl.pallas_call(
        functools.partial(fused_kernel, n, groups),
        out_shape=jax.ShapeDtypeStruct((rows, channels // groups), jnp.bfloat16),
        in_specs=[held] * 10,
        out_specs=vmem,
        scratch_shapes=[
            pltpu.SMEM(neighbours.shape, jnp.int32),
            pltpu.SMEM(radial_width.shape, jnp.float32),
            pltpu.VMEM(wavevectors.shape, jnp.int32),
            pltpu.VMEM(short_weight.shape, jnp.bfloat16),
            pltpu.VMEM(latent_weight.shape, jnp.bfloat16),
            pltpu.VMEM(mix_weight.shape, jnp.float32),
            pltpu.VMEM((1, latents), jnp.float32),
            pltpu.VMEM(out_weight.shape, jnp.bfloat16),
            pltpu.VMEM((n, 2, PIECES, rows // 2 // PIECES, channels), jnp.bfloat16),
            pltpu.VMEM((n, 3, rows), jnp.int32),
            pltpu.VMEM((channels, latents), jnp.bfloat16),
            pltpu.VMEM((2 * waves_each, latents), jnp.float32),
            pltpu.VMEM((local_kernels * rows, channels), jnp.float32),
            pltpu.VMEM((waves_each, 8), jnp.bfloat16),
            pltpu.VMEM((3, rows, BLOCK), jnp.int32),
            pltpu.VMEM((rows // BLOCK, blocks, BLOCK), jnp.float32),
            pltpu.VMEM((waves_each, latents), jnp.float32),
            pltpu.VMEM((rows, 2 * waves_each), jnp.bfloat16),
            pltpu.VMEM((local_kernels * rows, channels), jnp.bfloat16),
            pltpu.VMEM((groups, rows, channels // groups), jnp.bfloat16),
            pltpu.VMEM((groups, rows, channels // groups), jnp.bfloat16),
            *[pltpu.VMEM((2 * waves_each, rows), jnp.bfloat16) for _ in range(n)],
            *[pltpu.VMEM((local_kernels * rows, rows), jnp.bfloat16) for _ in range(n)],
            *[pltpu.VMEM((rows, latents), jnp.bfloat16) for _ in range(n)],
            dma((10,)),
            *[dma((lines * PIECES,)) for _ in range(5)],
            *[dma((n * PIECES,)) for _ in range(2)],
            *[dma((lines,)) for _ in range(5)],
            *[dma((groups,)) for _ in range(2)],
        ],
        compiler_params=pltpu.CompilerParams(
            collective_id=0, has_side_effects=True, vmem_limit_bytes=VMEM_LIMIT
        ),
    )(
        features.reshape(2, PIECES, rows // 2 // PIECES, channels),
        positions,
        neighbours,
        wavevectors,
        radial_width,
        short_weight,
        latent_weight,
        mix_weight,
        filter_rate.reshape(1, latents),
        out_weight,
    )


def layer(*arrays):
    features, wavevectors = arrays[0], arrays[3]
    n = lax.axis_size("atoms")
    groups = lax.axis_size("waves")
    rows = features.shape[0]
    reach_hops = -(-REACH // (rows // BLOCK))
    covers_all = 2 * reach_hops + 1 >= n
    if covers_all and groups == 4 and n % 2 == 0 and rows == 2 * BLOCK:
        if wavevectors.shape[1] % 512 == 0 and arrays[6].shape[1] % 128 == 0:
            return fused(*arrays)
    return local(*arrays)


def solution(mesh):
    placed = (
        P("atoms", None),
        P(None, "atoms"),
        P("atoms", None),
        P(None, "waves"),
        P("waves"),
        P("waves", None, None),
        P(),
        P(),
        P(),
        P(),
    )
    return jax.shard_map(
        layer, mesh=mesh, in_specs=placed, out_specs=P("atoms", "waves"), check_vma=False
    )
```

```python
import functools
import math

import jax
import jax.numpy as jnp
from jax import lax
from jax.experimental import pallas as pl
from jax.experimental.pallas import tpu as pltpu
from jax.sharding import PartitionSpec as P

K = 4096
RADIAL = 8
BLOCK = 128
NBR = 12
REACH = 7


cutoff = 0.5


def shifted(value, axis, steps):
    count = lax.axis_size(axis)
    pairs = [(source, (source + steps) % count) for source in range(count)]
    return lax.ppermute(value, axis, pairs)


def kernels(own_pos, near_pos, centers, radial_width):
    offsets = own_pos[:, None, :, None] - near_pos[:, :, None, :]
    offsets = jnp.mod(offsets, 65536)
    offsets = jnp.where(offsets >= 32768, offsets - 65536, offsets)
    coords = offsets.astype(jnp.float32) * (1.0 / 65536.0)
    dist_sq = jnp.sum(coords * coords, axis=0)
    distance = jnp.sqrt(dist_sq)
    smooth = jnp.where(
        dist_sq < cutoff * cutoff, jnp.square(1.0 - dist_sq / (cutoff * cutoff)), 0.0
    )
    shaped = (distance[None] - centers[:, None, None, None]) / radial_width[:, None, None, None]
    norm_scale = 1.0 / math.sqrt(NBR * BLOCK)
    return (jnp.exp(-jnp.square(shaped)) * smooth[None] * norm_scale).astype(jnp.bfloat16)


def phases_of(wavevectors, spots):
    phase_turn = (
        wavevectors[0][:, None] * spots[0][None, :]
        + wavevectors[1][:, None] * spots[1][None, :]
        + wavevectors[2][:, None] * spots[2][None, :]
    )
    phase_turn = jnp.mod(phase_turn, 65536)
    angles = phase_turn.astype(jnp.float32) * (2.0 * math.pi / 65536.0)
    return jnp.concatenate([jnp.cos(angles), jnp.sin(angles)], axis=0).astype(jnp.bfloat16)


def filter_gain(wavevectors, filter_rate):
    lengths = jnp.sum(wavevectors * wavevectors, axis=0).astype(jnp.float32)
    return jnp.exp(-lengths[:, None] * filter_rate[None, :])


def local(
    features,
    positions,
    neighbours,
    wavevectors,
    radial_width,
    short_weight,
    latent_weight,
    mix_weight,
    filter_rate,
    out_weight,
):
    row_count = features.shape[0]
    channels = features.shape[1]
    blocks_here = row_count // BLOCK
    atom_devices = lax.axis_size("atoms")
    total_blocks = blocks_here * atom_devices
    reach_hops = -(-REACH // blocks_here)
    window_feat = []
    window_pos = []
    for offset in range(-reach_hops, reach_hops + 1):
        if offset == 0:
            arrived = (features, positions)
        else:
            arrived = shifted((features, positions), "atoms", -offset)
        window_feat.append(arrived[0])
        window_pos.append(arrived[1])
    window_feat = jnp.concatenate(window_feat, axis=0).reshape(-1, BLOCK, channels)
    window_pos = jnp.concatenate(window_pos, axis=1).reshape(3, -1, BLOCK)
    first_block = lax.axis_index("atoms") * blocks_here - reach_hops * blocks_here
    local_near = jnp.mod(neighbours - first_block, total_blocks)
    own_pos = positions.reshape(3, blocks_here, BLOCK)
    local_kernels = radial_width.shape[0]
    kernel_ids = lax.axis_index("waves") * local_kernels + jnp.arange(
        local_kernels, dtype=jnp.int32
    )
    centers = cutoff * kernel_ids.astype(jnp.float32) / (RADIAL - 1)
    flat_weight = short_weight.reshape(local_kernels * channels, channels)

    def short_block(block_index):
        near_blocks = local_near[block_index]
        near_feat = jnp.stack(
            [lax.dynamic_index_in_dim(window_feat, near_blocks[j], 0, False) for j in range(NBR)]
        )
        near_pos = jnp.stack(
            [lax.dynamic_index_in_dim(window_pos, near_blocks[j], 1, False) for j in range(NBR)],
            axis=1,
        )
        weights = kernels(own_pos[:, block_index], near_pos, centers, radial_width)
        gathered = jnp.einsum(
            "rjia,jac->irc", weights, near_feat, preferred_element_type=jnp.float32
        )
        gathered = gathered.astype(jnp.bfloat16).reshape(BLOCK, local_kernels * channels)
        return jnp.dot(gathered, flat_weight, preferred_element_type=jnp.float32)

    short_range = lax.map(short_block, jnp.arange(blocks_here, dtype=jnp.int32)).reshape(
        row_count, channels
    )
    latent = jnp.dot(features, latent_weight, preferred_element_type=jnp.float32).astype(
        jnp.bfloat16
    )
    phases = phases_of(wavevectors, positions)
    partial_factors = jnp.dot(phases, latent, preferred_element_type=jnp.float32)
    gain = filter_gain(wavevectors, filter_rate)
    gain = jnp.concatenate([gain, gain], axis=0)
    norm_scale = 1.0 / math.sqrt(row_count * atom_devices)
    factors = lax.psum(partial_factors, "atoms")
    mixed = jnp.dot(factors, mix_weight, precision=lax.Precision.HIGHEST)
    filtered = (gain * mixed * norm_scale).astype(jnp.bfloat16)
    summed = lax.dot_general(
        phases, filtered, (((0,), (0,)), ((), ())), preferred_element_type=jnp.float32
    )
    summed = (summed * (1.0 / math.sqrt(K))).astype(jnp.bfloat16)
    long_range = jnp.dot(summed, out_weight, preferred_element_type=jnp.float32)
    combined = lax.psum_scatter(
        (short_range + long_range).astype(jnp.bfloat16), "waves", scatter_dimension=1, tiled=True
    )
    return combined


MESH = pl.DeviceIdType.MESH
PIECES = 4
VMEM_LIMIT = 67043328
HALF_SINE = (4.44526848, -7.31246730, 3.38876157)
HALF_COSINE = (1.41092230, -6.88237066, 4.96307940)
ROOT_LOG2E = math.sqrt(math.log2(math.e))


def cos_sin(turn):
    turn = turn - jnp.round(turn)
    square = turn * turn
    half_sine = HALF_SINE[-1] * square + HALF_SINE[-2]
    half_sine = (half_sine * square + HALF_SINE[0]) * turn
    half_cosine = HALF_COSINE[-1] * square + HALF_COSINE[-2]
    half_cosine = half_cosine * square + HALF_COSINE[0]
    return (
        (1.0 - half_sine * half_sine).astype(jnp.bfloat16),
        (half_sine * half_cosine).astype(jnp.bfloat16),
    )


def turned(rows):
    padded = jnp.concatenate([rows, jnp.zeros((5, rows.shape[1]), jnp.float32)], axis=0)
    return padded.T


def fused_kernel(
    n,
    groups,
    feat_ref,
    pos_ref,
    nbr_in,
    wave_in,
    width_in,
    short_in,
    latw_in,
    mix_in,
    rate_in,
    outw_in,
    out_ref,
    nbr_ref,
    width_ref,
    wave_ref,
    short_ref,
    latw_ref,
    mix_ref,
    rate_ref,
    outw_ref,
    feat_buf,
    pos_buf,
    fused_w,
    factors,
    gathered,
    wave_cols,
    spot_cols,
    keep_ref,
    gain_ref,
    own_turned,
    short_buf,
    send_buf,
    recv_buf,
    *rest,
):
    phase_refs, rest = rest[:n], rest[n:]
    weight_refs, rest = rest[:n], rest[n:]
    latent_refs, rest = rest[:n], rest[n:]
    (
        own_sem,
        line_up,
        line_down,
        line_recv,
        side_send,
        side_recv,
        fwd_send,
        fwd_recv,
        pos_up,
        pos_down,
        pos_line,
        pos_side_send,
        pos_side,
        msg_send,
        msg_recv,
    ) = rest
    me = lax.axis_index("atoms")
    group = lax.axis_index("waves")
    core, plane = lax.rem(group, 2), group // 2
    partner = group + 1 - 2 * core
    half, channels = feat_ref.shape[1] * feat_ref.shape[2], feat_ref.shape[3]
    rows = 2 * half
    blocks_here = rows // BLOCK
    local_kernels = short_ref.shape[0]
    waves_each = wave_ref.shape[1]
    lines = n // 2
    line, side = me // 2, lax.rem(me, 2)
    can_up, can_down = line < lines - 1, line > 0

    def ranked(rank):
        closest = jnp.minimum(line, lines - 1 - line)
        away = (rank + 1) // 2
        near_line = jnp.where(lax.rem(rank, 2) == 1, line - away, line + away)
        far_line = jnp.where(line < lines - 1 - line, rank, lines - 1 - rank)
        return jnp.where(rank <= 2 * closest, near_line, far_line)

    def remote(piece, send_sem, recv_sem, device):
        return pltpu.make_async_remote_copy(
            src_ref=piece[0],
            dst_ref=piece[1],
            send_sem=send_sem,
            recv_sem=recv_sem,
            device_id=device,
            device_id_type=MESH,
        )

    to_up, to_down = {"atoms": me + 2}, {"atoms": me - 2}
    to_side, to_core = {"atoms": me + 1 - 2 * side}, {"waves": partner}

    def feat_piece(shard_line, shard_side, which):
        place = feat_buf.at[2 * shard_line + shard_side, core, which]
        return place, place

    def own_piece(which):
        return feat_ref.at[core, which], feat_buf.at[me, core, which]

    def pos_piece(shard_line):
        place = pos_buf.at[2 * shard_line + side]
        return place, place

    own_pos_piece = (pos_ref, pos_buf.at[me])

    def up_copy(piece, slot):
        return remote(piece, line_up.at[slot], line_recv.at[slot], to_up)

    def down_copy(piece, slot):
        return remote(piece, line_down.at[slot], line_recv.at[slot], to_down)

    def side_copy(piece, slot):
        return remote(piece, side_send.at[slot], side_recv.at[slot], to_side)

    def forward_copy(shard_line, shard_side, which):
        slot = (2 * shard_line + shard_side) * PIECES + which
        return remote(
            feat_piece(shard_line, shard_side, which), fwd_send.at[slot], fwd_recv.at[slot], to_core
        )

    def pos_up_copy(piece, shard):
        return remote(piece, pos_up.at[shard], pos_line.at[shard], to_up)

    def pos_down_copy(piece, shard):
        return remote(piece, pos_down.at[shard], pos_line.at[shard], to_down)

    def pos_side_copy(piece, shard):
        return remote(piece, pos_side_send.at[shard], pos_side.at[shard], to_side)

    def msg_copy(step):
        target = lax.rem(group + step, groups)
        return remote(
            (send_buf.at[target], recv_buf.at[step]),
            msg_send.at[step],
            msg_recv.at[step],
            {"waves": target},
        )

    own_feat = pltpu.make_async_copy(feat_ref, feat_buf.at[me], own_sem.at[0])
    own_pos = pltpu.make_async_copy(pos_ref, pos_buf.at[me], own_sem.at[1])
    loads = [
        pltpu.make_async_copy(held, kept, own_sem.at[2 + which])
        for which, (held, kept) in enumerate(
            (
                (nbr_in, nbr_ref),
                (width_in, width_ref),
                (wave_in, wave_ref),
                (mix_in, mix_ref),
                (latw_in, latw_ref),
                (rate_in, rate_ref),
                (short_in, short_ref),
                (outw_in, outw_ref),
            )
        )
    ]

    barrier = pltpu.get_barrier_semaphore()

    @pl.when(can_up)
    def _():
        pl.semaphore_signal(barrier, inc=1, device_id=to_up, device_id_type=MESH)

    @pl.when(can_down)
    def _():
        pl.semaphore_signal(barrier, inc=1, device_id=to_down, device_id_type=MESH)

    pl.semaphore_signal(barrier, inc=1, device_id=to_side, device_id_type=MESH)
    for step in range(1, groups):
        pl.semaphore_signal(
            barrier,
            inc=1,
            device_id={"waves": lax.rem(group + step, groups)},
            device_id_type=MESH,
        )
    own_pos.start()
    for load in loads[:6]:
        load.start()
    own_feat.start()
    for load in loads[6:]:
        load.start()
    pl.semaphore_wait(
        barrier, groups + jnp.where(can_up, 1, 0) + jnp.where(can_down, 1, 0)
    )

    @pl.when(can_up)
    def _():
        pos_up_copy(own_pos_piece, line).start()

    @pl.when(can_down)
    def _():
        pos_down_copy(own_pos_piece, line).start()

    pos_side_copy(own_pos_piece, line).start()
    for which in range(PIECES):
        slot = line * PIECES + which

        @pl.when(can_up)
        def _():
            up_copy(own_piece(which), slot).start()

        @pl.when(can_down)
        def _():
            down_copy(own_piece(which), slot).start()

        side_copy(own_piece(which), slot).start()

    def pass_on(shard_line, which, upward):
        piece = feat_piece(shard_line, side, which)
        slot = shard_line * PIECES + which
        up_copy(piece, slot).wait_recv()
        if upward:

            @pl.when(can_up)
            def _():
                up_copy(piece, slot).start()

        else:

            @pl.when(can_down)
            def _():
                down_copy(piece, slot).start()

        side_copy(piece, slot).start()
        forward_copy(shard_line, side, which).start()

    def pass_pos(shard_line, upward):
        piece = pos_piece(shard_line)
        pos_up_copy(piece, shard_line).wait_recv()
        if upward:

            @pl.when(can_up)
            def _():
                pos_up_copy(piece, shard_line).start()

        else:

            @pl.when(can_down)
            def _():
                pos_down_copy(piece, shard_line).start()

        pos_side_copy(piece, shard_line).start()

    def at_distance(distance, act):
        @pl.when(line >= distance)
        def _():
            act(line - distance, True)

        @pl.when(line < lines - distance)
        def _():
            act(line + distance, False)

    wave_part = waves_each // PIECES
    row_part = rows // PIECES

    def phase_part(order, origin, part):
        position = pos_buf[origin]
        high = position >> 8
        low = position - (high << 8)
        split = jnp.concatenate(
            [
                high.astype(jnp.float32) * (1.0 / 256.0),
                low.astype(jnp.float32) * (1.0 / 65536.0),
                jnp.zeros((2, rows), jnp.float32),
            ],
            axis=0,
        ).astype(jnp.bfloat16)
        begin = pl.multiple_of(part * wave_part, wave_part)
        turn = jnp.dot(
            wave_cols[pl.ds(begin, wave_part), :], split, preferred_element_type=jnp.float32
        )
        cosine, sine = cos_sin(turn)
        phase_refs[order][pl.ds(begin, wave_part), :] = cosine
        after = pl.multiple_of(waves_each + begin, wave_part)
        phase_refs[order][pl.ds(after, wave_part), :] = sine

    def weight_part(order, origin, part):
        low = pl.multiple_of(part * row_part, row_part)
        near = pos_buf[origin] << 16
        block = (part * row_part) // BLOCK
        for near_block in range(blocks_here):
            lanes = slice(near_block * BLOCK, (near_block + 1) * BLOCK)
            total = None
            for axis in range(3):
                gap = spot_cols[axis, pl.ds(low, row_part), :] - near[axis : axis + 1, lanes]
                gap = gap.astype(jnp.float32)
                total = gap * gap if total is None else total + gap * gap
            distance = total * lax.rsqrt(jnp.maximum(total, 1.0))
            level = keep_ref[block, pl.ds(origin * blocks_here + near_block, 1), :]
            fall = level * (2.0**-64 / (cutoff * cutoff))
            smooth = jnp.maximum(level - total * fall, 0.0)
            smooth = smooth * smooth
            for kernel in range(local_kernels):
                shaped = distance * slopes[kernel] - shifts[kernel]
                weights = jnp.exp2(-(shaped * shaped)) * smooth
                weight_refs[order][
                    pl.ds(pl.multiple_of(kernel * rows + low, row_part), row_part), lanes
                ] = weights.astype(jnp.bfloat16)

    def make_latent(order, origin):
        feats = feat_buf[origin].reshape(rows, channels)
        latent_refs[order][...] = jnp.dot(
            feats, fused_w[...], preferred_element_type=jnp.float32
        ).astype(jnp.bfloat16)

    def use_part(shards, part):
        size = 2 * waves_each // PIECES
        begin = pl.ds(pl.multiple_of(part * size, size), size)
        total = factors[begin, :]
        for order, _ in shards:
            total += jnp.dot(
                phase_refs[order][begin, :], latent_refs[order][...], preferred_element_type=jnp.float32
            )
        factors[begin, :] = total
        size = local_kernels * rows // PIECES
        begin = pl.ds(pl.multiple_of(part * size, size), size)
        total = gathered[begin, :]
        for order, origin in shards:
            total += jnp.dot(
                weight_refs[order][begin, :],
                feat_buf[origin].reshape(rows, channels),
                preferred_element_type=jnp.float32,
            )
        gathered[begin, :] = total

    own_pos.wait()
    for load in loads[:6]:
        load.wait()
    slopes, shifts = [], []
    for kernel in range(local_kernels):
        center = (group * local_kernels + kernel).astype(jnp.float32) * (cutoff / (RADIAL - 1))
        slope = ROOT_LOG2E / width_ref[kernel]
        slopes.append(slope * 2.0**-32)
        shifts.append(slope * center)
    spots = turned(pos_buf[me].astype(jnp.float32))
    for axis in range(3):
        column = jnp.broadcast_to(spots[:, axis : axis + 1], (rows, BLOCK))
        spot_cols[axis] = column.astype(jnp.int32) << 16
    number = lax.broadcasted_iota(jnp.int32, (n * blocks_here, BLOCK), 0)
    for block in range(blocks_here):
        level = jnp.zeros((n * blocks_here, BLOCK), jnp.float32)
        for slot in range(NBR):
            level = jnp.where(number == nbr_ref[block, slot], (NBR * BLOCK) ** -0.25, level)
        keep_ref[block] = level
    waves = turned(wave_ref[...].astype(jnp.float32))
    wave_cols[...] = jnp.concatenate(
        [waves[:, :3], waves[:, :3], jnp.zeros((waves_each, 2), jnp.float32)], axis=1
    ).astype(jnp.bfloat16)
    lengths = waves[:, :1] * waves[:, :1] + waves[:, 1:2] * waves[:, 1:2]
    lengths = lengths + waves[:, 2:3] * waves[:, 2:3]
    gain_ref[...] = jnp.exp(-lengths * rate_ref[...]) * (1.0 / math.sqrt(rows * n * K))
    mix_high = mix_ref[...].astype(jnp.bfloat16)
    mix_low = (mix_ref[...] - mix_high.astype(jnp.float32)).astype(jnp.bfloat16)
    fused_w[...] = (
        jnp.dot(latw_ref[...], mix_high, preferred_element_type=jnp.float32)
        + jnp.dot(latw_ref[...], mix_low, preferred_element_type=jnp.float32)
    ).astype(jnp.bfloat16)
    factors[...] = jnp.zeros_like(factors)
    gathered[...] = jnp.zeros_like(gathered)

    def own_part(part, carry):
        phase_part(0, me, part)
        weight_part(0, me, part)
        return carry

    lax.fori_loop(0, PIECES, own_part, 0, unroll=True)
    own_feat.wait()

    own_side = [(0, me)] + [(2 * r - 1, 2 * ranked(r) + side) for r in range(1, lines)]
    other_side = [(2 * r + 2 if r < lines - 1 else n - 1, 2 * ranked(r) + 1 - side) for r in range(lines)]

    def wait_forwards(shard_line, shard_side):
        for which in range(PIECES):
            forward_copy(shard_line, shard_side, which).wait_recv()

    def round_of(rank):
        made = []
        used = []
        if rank < lines:
            at_distance(rank, pass_pos)
            made.append(own_side[rank])
        pos_side_copy(pos_piece(ranked(rank - 1)), ranked(rank - 1)).wait_recv()
        made.append(other_side[rank - 1])
        used.append(own_side[rank - 1])
        if rank > 1:
            used.append(other_side[rank - 2])

        def one(part, carry):
            if rank < lines:
                at_distance(rank, lambda shard_line, upward: pass_on(shard_line, part, upward))
            shard_line = ranked(rank - 1)
            slot = shard_line * PIECES + part
            side_copy(feat_piece(shard_line, 1 - side, part), slot).wait_recv()
            forward_copy(shard_line, 1 - side, part).start()

            @pl.when(part == 0)
            def _():
                if rank > 1:
                    wait_forwards(ranked(rank - 1), side)
                    wait_forwards(ranked(rank - 2), 1 - side)
                for held in used:
                    make_latent(*held)

            use_part(used, part)
            for order, origin in made:
                phase_part(order, origin, part)
                weight_part(order, origin, part)
            if rank == 1:
                size = 2 * waves_each // PIECES
                begin = pl.ds(pl.multiple_of(part * size, size), size)
                own_turned[:, begin] = phase_refs[0][begin, :].T
            return carry

        lax.fori_loop(0, PIECES, one, 0)

    for rank in range(1, lines + 1):
        round_of(rank)
    wait_forwards(ranked(lines - 1), 1 - side)
    order, origin = other_side[lines - 1]
    make_latent(order, origin)
    size = waves_each // 2
    reduced = jnp.zeros((rows, gain_ref.shape[1]), jnp.float32)
    for part in range(4):
        begin = slice(part * size, (part + 1) * size)
        total = factors[begin, :] + jnp.dot(
            phase_refs[order][begin, :], latent_refs[order][...], preferred_element_type=jnp.float32
        )
        low = (part % 2) * size
        filtered = (total * gain_ref[low : low + size, :]).astype(jnp.bfloat16)
        reduced += jnp.dot(own_turned[:, begin], filtered, preferred_element_type=jnp.float32)
    reduced = reduced.astype(jnp.bfloat16)
    size = local_kernels * rows // PIECES
    for part in range(PIECES):
        begin = slice(part * size, (part + 1) * size)
        total = gathered[begin, :] + jnp.dot(
            weight_refs[order][begin, :],
            feat_buf[origin].reshape(rows, channels),
            preferred_element_type=jnp.float32,
        )
        short_buf[begin, :] = total.astype(jnp.bfloat16)
    for load in loads[6:]:
        load.wait()
    width = out_ref.shape[1]

    def part_sum(chip):
        columns = pl.ds(pl.multiple_of(chip * 2 * width, 2 * width), 2 * width)
        total = jnp.dot(reduced, outw_ref[:, columns], preferred_element_type=jnp.float32)
        for kernel in range(local_kernels):
            total += jnp.dot(
                short_buf[kernel * rows : (kernel + 1) * rows],
                short_ref[kernel, :, columns],
                preferred_element_type=jnp.float32,
            )
        return total

    far = part_sum(1 - plane)
    left, right = far[:, :width], far[:, width:]
    send_buf[2 * (1 - plane) + core] = jnp.where(core == 0, left, right).astype(jnp.bfloat16)
    msg_copy(2).start()
    send_buf[2 * (1 - plane) + 1 - core] = jnp.where(core == 0, right, left).astype(jnp.bfloat16)
    msg_copy(3 - 2 * core).start()
    near = part_sum(plane)
    first, second = near[:, :width], near[:, width:]
    send_buf[partner] = jnp.where(core == 0, second, first).astype(jnp.bfloat16)
    msg_copy(1 + 2 * core).start()
    total = jnp.where(core == 0, first, second)
    def finish(shard_line, carry):
        piece = pos_piece(shard_line)

        @pl.when((shard_line <= line) & can_up)
        def _():
            pos_up_copy(piece, shard_line).wait_send()

        @pl.when((shard_line >= line) & can_down)
        def _():
            pos_down_copy(piece, shard_line).wait_send()

        pos_side_copy(piece, shard_line).wait_send()
        for which in range(PIECES):
            piece = feat_piece(shard_line, side, which)
            slot = shard_line * PIECES + which

            @pl.when((shard_line <= line) & can_up)
            def _():
                up_copy(piece, slot).wait_send()

            @pl.when((shard_line >= line) & can_down)
            def _():
                down_copy(piece, slot).wait_send()

            side_copy(piece, slot).wait_send()
            forward_copy(shard_line, 1 - side, which).wait_send()

            @pl.when(shard_line != line)
            def _():
                forward_copy(shard_line, side, which).wait_send()

        return carry

    lax.fori_loop(0, lines, finish, 0)
    for step in range(1, groups):
        msg_copy(step).wait_recv()
        total += recv_buf[step].astype(jnp.float32)
    out_ref[...] = total.astype(out_ref.dtype)

    for step in range(1, groups):
        msg_copy(step).wait_send()


def fused(
    features,
    positions,
    neighbours,
    wavevectors,
    radial_width,
    short_weight,
    latent_weight,
    mix_weight,
    filter_rate,
    out_weight,
):
    n = lax.axis_size("atoms")
    groups = lax.axis_size("waves")
    rows, channels = features.shape
    latents = latent_weight.shape[1]
    waves_each = wavevectors.shape[1]
    local_kernels = radial_width.shape[0]
    blocks = n * rows // BLOCK
    vmem = pl.BlockSpec(memory_space=pltpu.VMEM)
    held = pl.BlockSpec(memory_space=pl.ANY)
    dma = pltpu.SemaphoreType.DMA
    lines = n // 2
    return pl.pallas_call(
        functools.partial(fused_kernel, n, groups),
        out_shape=jax.ShapeDtypeStruct((rows, channels // groups), jnp.bfloat16),
        in_specs=[held] * 10,
        out_specs=vmem,
        scratch_shapes=[
            pltpu.SMEM(neighbours.shape, jnp.int32),
            pltpu.SMEM(radial_width.shape, jnp.float32),
            pltpu.VMEM(wavevectors.shape, jnp.int32),
            pltpu.VMEM(short_weight.shape, jnp.bfloat16),
            pltpu.VMEM(latent_weight.shape, jnp.bfloat16),
            pltpu.VMEM(mix_weight.shape, jnp.float32),
            pltpu.VMEM((1, latents), jnp.float32),
            pltpu.VMEM(out_weight.shape, jnp.bfloat16),
            pltpu.VMEM((n, 2, PIECES, rows // 2 // PIECES, channels), jnp.bfloat16),
            pltpu.VMEM((n, 3, rows), jnp.int32),
            pltpu.VMEM((channels, latents), jnp.bfloat16),
            pltpu.VMEM((2 * waves_each, latents), jnp.float32),
            pltpu.VMEM((local_kernels * rows, channels), jnp.float32),
            pltpu.VMEM((waves_each, 8), jnp.bfloat16),
            pltpu.VMEM((3, rows, BLOCK), jnp.int32),
            pltpu.VMEM((rows // BLOCK, blocks, BLOCK), jnp.float32),
            pltpu.VMEM((waves_each, latents), jnp.float32),
            pltpu.VMEM((rows, 2 * waves_each), jnp.bfloat16),
            pltpu.VMEM((local_kernels * rows, channels), jnp.bfloat16),
            pltpu.VMEM((groups, rows, channels // groups), jnp.bfloat16),
            pltpu.VMEM((groups, rows, channels // groups), jnp.bfloat16),
            *[pltpu.VMEM((2 * waves_each, rows), jnp.bfloat16) for _ in range(n)],
            *[pltpu.VMEM((local_kernels * rows, rows), jnp.bfloat16) for _ in range(n)],
            *[pltpu.VMEM((rows, latents), jnp.bfloat16) for _ in range(n)],
            dma((10,)),
            *[dma((lines * PIECES,)) for _ in range(5)],
            *[dma((n * PIECES,)) for _ in range(2)],
            *[dma((lines,)) for _ in range(5)],
            *[dma((groups,)) for _ in range(2)],
        ],
        compiler_params=pltpu.CompilerParams(
            collective_id=0, has_side_effects=True, vmem_limit_bytes=VMEM_LIMIT
        ),
    )(
        features.reshape(2, PIECES, rows // 2 // PIECES, channels),
        positions,
        neighbours,
        wavevectors,
        radial_width,
        short_weight,
        latent_weight,
        mix_weight,
        filter_rate.reshape(1, latents),
        out_weight,
    )


def layer(*arrays):
    features, wavevectors = arrays[0], arrays[3]
    n = lax.axis_size("atoms")
    groups = lax.axis_size("waves")
    rows = features.shape[0]
    reach_hops = -(-REACH // (rows // BLOCK))
    covers_all = 2 * reach_hops + 1 >= n
    if covers_all and groups == 4 and n % 2 == 0 and rows == 2 * BLOCK:
        if wavevectors.shape[1] % 512 == 0 and arrays[6].shape[1] % 128 == 0:
            return fused(*arrays)
    return local(*arrays)


def solution(mesh):
    placed = (
        P("atoms", None),
        P(None, "atoms"),
        P("atoms", None),
        P(None, "waves"),
        P("waves"),
        P("waves", None, None),
        P(),
        P(),
        P(),
        P(),
    )
    return jax.shard_map(
        layer, mesh=mesh, in_specs=placed, out_specs=P("atoms", "waves"), check_vma=False
    )
```
